32 devices in a mesh: fsdp: 16 (over z, y, core), pair: 2 (over x).
Axes of the slice: x: 2, y: 2, z: 4, core: 2. Of those that a mesh axis runs over, the one named last changes fastest.
Arguments:
- tokens: bfloat16 [2, 128, 32, 2048], P(None, ('fsdp', 'pair')), may hold values from -6 to 6
- cotangent: bfloat16 [2, 128, 32, 2048], P(None, ('fsdp', 'pair')), may hold values from -6 to 6
- lengths: int32 [2, 32], replicated, may hold values from 65 to 128, as said below
- order: int32 [2, 32], replicated, may hold values from 0 to 31, each once within a row
- norm_gain: bfloat16 [2048], P(('fsdp', 'pair')), may hold values from 0.5 to 1.5
- w_query: bfloat16 [2048, 256], P(('fsdp', 'pair')), may hold values from -0.125 to 0.125
- w_key: bfloat16 [2048, 256], P(('fsdp', 'pair')), may hold values from -0.125 to 0.125
- w_value: bfloat16 [2048, 2048], P(('fsdp', 'pair')), may hold values from -0.125 to 0.125
- w_out: bfloat16 [2048, 2048], P(('fsdp', 'pair')), may hold values from -1 to 1
- mlp_gain: bfloat16 [2048], P(('fsdp', 'pair')), may hold values from 0.5 to 1.5
- w_gate: bfloat16 [2048, 5632], P(('fsdp', 'pair')), may hold values from -0.125 to 0.125
- w_up: bfloat16 [2048, 5632], P(('fsdp', 'pair')), may hold values from -0.125 to 0.125
- w_down: bfloat16 [5632, 2048], P(('fsdp', 'pair')), may hold values from -0.078125 to 0.078125
Outputs:
- activations: bfloat16 [2, 128, 32, 2048], P(None, ('fsdp', 'pair'))
- input_grad: bfloat16 [2, 128, 32, 2048], P(None, ('fsdp', 'pair'))
- grad_norm_gain: float32 [2048], P(('fsdp', 'pair'))
- grad_query: float32 [2048, 256], P(('fsdp', 'pair'))
- grad_key: float32 [2048, 256], P(('fsdp', 'pair'))
- grad_value: float32 [2048, 2048], P(('fsdp', 'pair'))
- grad_out: float32 [2048, 2048], P(('fsdp', 'pair'))
- grad_mlp_gain: float32 [2048], P(('fsdp', 'pair'))
- grad_gate: float32 [2048, 5632], P(('fsdp', 'pair'))
- grad_up: float32 [2048, 5632], P(('fsdp', 'pair'))
- grad_down: float32 [5632, 2048], P(('fsdp', 'pair'))
The draws below stay inside these ranges and needn't reach their ends.
Inputs may be any that keep to these rules, and one draw needn't show every extreme that they name: lengths[m, j] counts the live positions of sequence order[m, j]; in every micro-batch some sequence has all 128 positions live. Each row order[m, :] is a permutation of the sequences.
All inputs are finite; a program needn't handle non-finite values.
Results may differ from the reference program's by a relative error of at most 0.013.
Values may be sent and summed in bfloat16 or wider, within the bound.
A program may use at most 448 MiB of HBM per device.

```python
import jax
import jax.numpy as jnp
from jax import lax

D = 2048
FF = 5632
HEADS = 16
SEQ = 128
MB = 2
QK = 256
NSEQ = 32


def draw_lengths(key, part):
    first_key, second_key = jax.random.split(key)
    drawn = jax.random.randint(first_key, (MB, NSEQ), SEQ // 2 + 1, SEQ + 1)
    full_slot = jax.random.randint(second_key, (MB, 1), 0, NSEQ)
    columns = jnp.arange(NSEQ)[None, :]
    return jnp.where(columns == full_slot, SEQ, drawn).astype(jnp.int32)


def block_levels(stream_key, dims, cuts, low, top_value):
    loudness = 1.0
    for dim, parts in cuts:
        steps = jax.random.uniform(jax.random.fold_in(jax.random.fold_in(stream_key, 6), dim), (parts,), jnp.float32, low / len(cuts), top_value / len(cuts))
        loudness = loudness * jnp.repeat(jnp.exp(steps), dims[dim] // parts).reshape((-1,) + (1,) * (len(dims) - 1 - dim))
    return loudness


def normal_values(rng, dims, spread, limit, shards=(), held_as=jnp.bfloat16):
    loudness = block_levels(rng, dims, shards, -0.22, 0.18) if shards else 1.0
    values = jax.random.normal(rng, dims, jnp.float32) * spread * loudness
    return jnp.minimum(jnp.maximum(values, -limit), limit).astype(held_as)


def setup_inputs(seed: int = 0) -> dict:
    key_list = jax.random.split(jax.random.key(seed), 14)
    tokens = normal_values(key_list[0], (MB, SEQ, NSEQ, D), 1.0, 6.0, ((1, 32),))
    cotangent = normal_values(key_list[1], (MB, SEQ, NSEQ, D), 1.0, 6.0, ((1, 32),))
    lengths = draw_lengths(jax.random.fold_in(key_list[13], 71), 0)
    order = jax.vmap(lambda own: jax.random.permutation(own, NSEQ))(jax.random.split(key_list[3], MB)).reshape((MB, NSEQ)).astype(jnp.int32)
    norm_gain = jnp.clip(1.0 + 0.1 * jax.random.normal(key_list[4], (D,), jnp.float32), 0.5, 1.5).astype(jnp.bfloat16)
    w_query = normal_values(key_list[5], (D, QK), D ** -0.5, 0.125, ((0, 32),))
    w_key = normal_values(key_list[6], (D, QK), D ** -0.5, 0.125, ((0, 32),))
    w_value = normal_values(key_list[7], (D, D), D ** -0.5, 0.125, ((0, 32),))
    w_out = normal_values(key_list[8], (D, D), (D // 64) ** -0.5, 1.0, ((0, 32),))
    mlp_gain = jnp.clip(1.0 + 0.1 * jax.random.normal(key_list[9], (D,), jnp.float32), 0.5, 1.5).astype(jnp.bfloat16)
    w_gate = normal_values(key_list[10], (D, FF), D ** -0.5, 0.125, ((0, 32),))
    w_up = normal_values(key_list[11], (D, FF), D ** -0.5, 0.125, ((0, 32),))
    w_down = normal_values(key_list[12], (FF, D), FF ** -0.5, 0.078125, ((0, 32),))
    return {"tokens": tokens, "cotangent": cotangent, "lengths": lengths, "order": order, "norm_gain": norm_gain, "w_query": w_query, "w_key": w_key, "w_value": w_value, "w_out": w_out, "mlp_gain": mlp_gain, "w_gate": w_gate, "w_up": w_up, "w_down": w_down}


PRECISE = lax.Precision.HIGHEST
EPSILON = 1e-06

@jax.custom_vjp
def low(v):
    return lax.optimization_barrier(v.astype(jnp.bfloat16)).astype(jnp.float32)

@jax.custom_vjp
def low_back(v):
    return v

def low_keep(v):
    return (low(v), None)

def low_pass(kept, grad):
    return (grad,)

def back_keep(v):
    return (v, None)

def back_low(kept, grad):
    return (low(grad),)
low.defvjp(low_keep, low_pass)
low_back.defvjp(back_keep, back_low)

def matmul(left, right):
    return jnp.einsum('bsd,de->bse', left, right, precision=PRECISE)

def rms_norm(rows_in, gain):
    factor = lax.rsqrt(lax.optimization_barrier(jnp.mean(rows_in * rows_in, -1, keepdims=True)) + EPSILON)
    return rows_in * factor * gain

def block(start, seq_lens, norm_gain, w_query, w_key, w_value, w_out, mlp_gain, w_gate, w_up, w_down):
    batch_count, seq_len, model_width = start.shape
    hidden1 = low(rms_norm(start, norm_gain))
    query = low_back(low(matmul(hidden1, w_query)))
    keys = low_back(low(matmul(hidden1, w_key)))
    values = low_back(low(matmul(hidden1, w_value)))
    features = query.shape[-1] // HEADS
    query_heads = query.reshape(batch_count, seq_len, HEADS, features)
    key_heads = keys.reshape(batch_count, seq_len, HEADS, features)
    scores = jnp.einsum('bihe,bjhe->bhij', query_heads, key_heads, precision=PRECISE) * features ** (-0.5)
    row_ids = jnp.arange(seq_len)[:, None]
    col_ids = jnp.arange(seq_len)[None, :]
    key_mask = (col_ids <= row_ids)[None] & (col_ids[None] < seq_lens[:, None, None])
    kernel = jnp.where(key_mask[:, None], 1.0 + scores + 0.5 * scores * scores, 0.0)
    probs = low(kernel / lax.optimization_barrier(jnp.sum(kernel, -1, keepdims=True)))
    value_heads = values.reshape(batch_count, seq_len, HEADS, model_width // HEADS)
    mixed = jnp.einsum('bhij,bjhe->bihe', probs, value_heads, precision=PRECISE)
    attended = low_back(low(mixed.reshape(batch_count, seq_len, model_width)))
    resid = start + low_back(matmul(attended, w_out))
    hidden2 = low(rms_norm(resid, mlp_gain))
    gate_pre = low_back(matmul(hidden2, w_gate))
    up_pre = low_back(matmul(hidden2, w_up))
    inner = low(jax.nn.silu(gate_pre) * up_pre)
    return resid + matmul(inner, w_down)

def reference(tokens, cotangent, lengths, order, norm_gain, w_query, w_key, w_value, w_out, mlp_gain, w_gate, w_up, w_down):
    weights = tuple((weight.astype(jnp.float32) for weight in (norm_gain, w_query, w_key, w_value, w_out, mlp_gain, w_gate, w_up, w_down)))
    seq_len = tokens.shape[1]

    def one_batch(totals, items):
        batch_tokens, batch_cots, dealt_lens, permuted = items
        seq_lens = jnp.zeros(permuted.shape, jnp.int32).at[permuted].set(dealt_lens.astype(jnp.int32))
        start = jnp.transpose(batch_tokens.astype(jnp.float32), (1, 0, 2))
        result, pullback = jax.vjp(lambda rows_in, *params: block(rows_in, seq_lens, *params), start, *weights)
        live_rows = jnp.arange(seq_len)[None, :, None] < seq_lens[:, None, None]
        seed_grad = jnp.where(live_rows, jnp.transpose(batch_cots.astype(jnp.float32), (1, 0, 2)), 0.0)
        grads = pullback(seed_grad)
        totals = tuple((first + second for first, second in zip(totals, grads[1:])))
        outputs = (jnp.transpose(result, (1, 0, 2)).astype(jnp.bfloat16), jnp.transpose(grads[0], (1, 0, 2)).astype(jnp.bfloat16))
        return (totals, outputs)
    zero_grads = tuple((jnp.zeros(weight.shape, jnp.float32) for weight in weights))
    totals, stacked = lax.scan(one_batch, zero_grads, (tokens, cotangent, lengths, order))
    return (stacked[0], stacked[1], totals[0], totals[1], totals[2], totals[3], totals[4], totals[5], totals[6], totals[7], totals[8])
```

```python
import functools
import math

import jax
import jax.numpy as jnp
from jax import lax
from jax.experimental import pallas as pl
from jax.experimental.pallas import tpu as pltpu
from jax.sharding import Mesh
from jax.sharding import PartitionSpec as P

HEADS = 16


PRECISE = lax.Precision.HIGHEST
EPSILON = 1e-06


def for_sending(shard):

    def short(part):
        return part.astype(jnp.bfloat16) if part.dtype == jnp.float32 else part

    return jax.tree.map(short, shard)


def take_rows(left, right):
    return lax.dot_general(
        left, right, (((0,), (0,)), ((), ())), preferred_element_type=jnp.float32
    )


def back_cols(left, right):
    return lax.dot_general(
        left, right, (((1,), (1,)), ((), ())), preferred_element_type=jnp.float32
    )


def kernel_terms(query, keys, length):
    seq_len = query.shape[0]
    features = query.shape[1] // HEADS
    query_heads = query.reshape(seq_len, HEADS, features)
    key_heads = keys.reshape(seq_len, HEADS, features)
    scores = jnp.einsum(
        "ihe,jhe->hij", query_heads, key_heads, preferred_element_type=jnp.float32
    ) * features ** (-0.5)
    row_ids = lax.broadcasted_iota(jnp.int32, (seq_len, seq_len), 0)
    col_ids = lax.broadcasted_iota(jnp.int32, (seq_len, seq_len), 1)
    key_mask = (col_ids <= row_ids) & (col_ids < length)
    kernel = jnp.where(key_mask[None], 1.0 + scores + 0.5 * scores * scores, 0.0)
    return (kernel, key_mask, scores)


def forward_one(start_rows, cot_rows, length, weights):
    norm_gain, w_query, w_key, w_value, w_out, mlp_gain, w_gate, w_up, w_down = weights
    seq_len, model_width = start_rows.shape
    start = start_rows.astype(jnp.float32)
    scale1 = lax.rsqrt(jnp.mean(start * start, -1, keepdims=True) + EPSILON)
    normed1 = start * scale1
    hidden1 = (normed1 * norm_gain.astype(jnp.float32)).astype(jnp.bfloat16)
    query = jnp.dot(hidden1, w_query, preferred_element_type=jnp.float32).astype(jnp.bfloat16)
    keys = jnp.dot(hidden1, w_key, preferred_element_type=jnp.float32).astype(jnp.bfloat16)
    values = jnp.dot(hidden1, w_value, preferred_element_type=jnp.float32).astype(jnp.bfloat16)
    kernel, key_mask, scores = kernel_terms(query, keys, length)
    denom = jnp.sum(kernel, -1)
    probs = (kernel / denom[..., None]).astype(jnp.bfloat16)
    value_heads = values.reshape(seq_len, HEADS, model_width // HEADS)
    mixed = jnp.einsum("hij,jhe->ihe", probs, value_heads, preferred_element_type=jnp.float32)
    attended = mixed.reshape(seq_len, model_width).astype(jnp.bfloat16)
    resid = start + jnp.dot(attended, w_out, preferred_element_type=jnp.float32)
    scale2 = lax.rsqrt(jnp.mean(resid * resid, -1, keepdims=True) + EPSILON)
    normed2 = resid * scale2
    hidden2 = (normed2 * mlp_gain.astype(jnp.float32)).astype(jnp.bfloat16)
    gate_pre = jnp.dot(hidden2, w_gate, preferred_element_type=jnp.float32)
    up_pre = jnp.dot(hidden2, w_up, preferred_element_type=jnp.float32)
    inner = (gate_pre * jax.nn.sigmoid(gate_pre) * up_pre).astype(jnp.bfloat16)
    result = resid + jnp.dot(inner, w_down, preferred_element_type=jnp.float32)
    saved = (
        cot_rows,
        length,
        normed1,
        scale1,
        hidden1,
        query,
        keys,
        values,
        denom,
        attended,
        normed2,
        scale2,
        hidden2,
        gate_pre,
        up_pre,
        inner,
    )
    return (result, saved)


def backward_one(saved, weights):
    norm_gain, w_query, w_key, w_value, w_out, mlp_gain, w_gate, w_up, w_down = weights
    (
        cot_rows,
        length,
        normed1,
        scale1,
        hidden1,
        query,
        keys,
        values,
        denom,
        attended,
        normed2,
        scale2,
        hidden2,
        gate_pre,
        up_pre,
        inner,
    ) = saved
    seq_len, model_width = normed1.shape
    live_rows = lax.broadcasted_iota(jnp.int32, (seq_len, 1), 0) < length
    d_out = jnp.where(live_rows, cot_rows, jnp.zeros_like(cot_rows))
    d_inner = back_cols(d_out, w_down)
    sigma = jax.nn.sigmoid(gate_pre)
    d_gate = (d_inner * up_pre * sigma * (1.0 + gate_pre * (1.0 - sigma))).astype(jnp.bfloat16)
    d_up = (d_inner * gate_pre * sigma).astype(jnp.bfloat16)
    d_hidden2 = back_cols(d_gate, w_gate) + back_cols(d_up, w_up)
    g_mlp = jnp.sum(d_hidden2 * normed2, 0)
    d_norm2 = d_hidden2 * mlp_gain.astype(jnp.float32)
    d_resid = d_out.astype(jnp.float32) + scale2 * (
        d_norm2 - normed2 * jnp.mean(d_norm2 * normed2, -1, keepdims=True)
    )
    d_branch = d_resid.astype(jnp.bfloat16)
    d_attended = back_cols(d_branch, w_out).astype(jnp.bfloat16)
    kernel, key_mask, scores = kernel_terms(query, keys, length)
    probs = kernel / denom[..., None]
    value_heads = values.reshape(seq_len, HEADS, model_width // HEADS)
    grad_heads = d_attended.reshape(seq_len, HEADS, model_width // HEADS)
    d_probs = jnp.einsum(
        "ihe,jhe->hij", grad_heads, value_heads, preferred_element_type=jnp.float32
    )
    d_values = jnp.einsum(
        "hij,ihe->jhe", probs.astype(jnp.bfloat16), grad_heads, preferred_element_type=jnp.float32
    )
    d_values = d_values.reshape(seq_len, model_width).astype(jnp.bfloat16)
    d_kernel = (d_probs - jnp.sum(d_probs * probs, -1, keepdims=True)) / denom[..., None]
    features = query.shape[1] // HEADS
    d_scores = jnp.where(key_mask[None], d_kernel * (1.0 + scores), 0.0) * features ** (-0.5)
    query_heads = query.reshape(seq_len, HEADS, features).astype(jnp.float32)
    key_heads = keys.reshape(seq_len, HEADS, features).astype(jnp.float32)
    d_query = (
        jnp.einsum("hij,jhe->ihe", d_scores, key_heads, precision=PRECISE)
        .reshape(seq_len, -1)
        .astype(jnp.bfloat16)
    )
    d_keys = (
        jnp.einsum("hij,ihe->jhe", d_scores, query_heads, precision=PRECISE)
        .reshape(seq_len, -1)
        .astype(jnp.bfloat16)
    )
    d_hidden1 = (
        back_cols(d_query, w_query) + back_cols(d_keys, w_key) + back_cols(d_values, w_value)
    )
    g_norm = jnp.sum(d_hidden1 * normed1, 0)
    d_norm1 = d_hidden1 * norm_gain.astype(jnp.float32)
    d_start = d_resid + scale1 * (
        d_norm1 - normed1 * jnp.mean(d_norm1 * normed1, -1, keepdims=True)
    )
    record_rows = (
        hidden1,
        d_query,
        d_keys,
        d_values,
        attended,
        d_branch,
        hidden2,
        d_gate,
        d_up,
        inner,
        d_out,
    )
    return (d_start.astype(jnp.bfloat16), record_rows, (g_norm, g_mlp))


def owner_sums(terms):
    arrived = jax.tree.map(
        lambda part, own: part.astype(own.dtype),
        lax.all_to_all(
            for_sending(terms), ("fsdp", "pair"), split_axis=0, concat_axis=0, tiled=True
        ),
        terms,
    )
    count = lax.axis_size(("fsdp", "pair"))
    return tuple(
        (
            jnp.sum(piece.reshape(count, piece.shape[0] // count, piece.shape[1]), 0)
            for piece in arrived
        )
    )


def restore(arrived, permuted):
    inverse = (
        jnp.zeros_like(permuted).at[permuted].set(jnp.arange(permuted.shape[0], dtype=jnp.int32))
    )
    return jnp.take(arrived, inverse, axis=1)


def fetch_backward(owned):
    return (
        lax.all_gather(owned[0], ("fsdp", "pair"), axis=0, tiled=True),
        lax.all_gather(owned[1], ("fsdp", "pair"), axis=0, tiled=True),
        lax.all_gather(owned[2], ("fsdp", "pair"), axis=0, tiled=True),
        lax.all_gather(owned[3], ("fsdp", "pair"), axis=0, tiled=True),
        lax.all_gather(owned[4], ("fsdp", "pair"), axis=0, tiled=True),
        lax.all_gather(owned[5], ("fsdp", "pair"), axis=0, tiled=True),
        lax.all_gather(owned[6], ("fsdp", "pair"), axis=0, tiled=True),
        lax.all_gather(owned[7], ("fsdp", "pair"), axis=0, tiled=True),
        lax.all_gather(owned[8], ("fsdp", "pair"), axis=0, tiled=True),
    )


def add_tuples(first_tuple, second_tuple):
    return tuple((first + second for first, second in zip(first_tuple, second_tuple)))


def on_device(
    tokens,
    cotangent,
    lengths,
    order,
    norm_gain,
    w_query,
    w_key,
    w_value,
    w_out,
    mlp_gain,
    w_gate,
    w_up,
    w_down,
):
    owned = (norm_gain, w_query, w_key, w_value, w_out, mlp_gain, w_gate, w_up, w_down)
    batches = tokens.shape[0]
    device_index = lax.axis_index(("fsdp", "pair"))
    stored = []
    outputs = []
    for micro_step in range(batches):
        weights = (
            lax.all_gather(owned[0], ("fsdp", "pair"), axis=0, tiled=True),
            lax.all_gather(owned[1], ("fsdp", "pair"), axis=0, tiled=True),
            lax.all_gather(owned[2], ("fsdp", "pair"), axis=0, tiled=True),
            lax.all_gather(owned[3], ("fsdp", "pair"), axis=0, tiled=True),
            lax.all_gather(owned[4], ("fsdp", "pair"), axis=0, tiled=True),
            lax.all_gather(owned[5], ("fsdp", "pair"), axis=0, tiled=True),
            lax.all_gather(owned[6], ("fsdp", "pair"), axis=0, tiled=True),
            lax.all_gather(owned[7], ("fsdp", "pair"), axis=0, tiled=True),
            lax.all_gather(owned[8], ("fsdp", "pair"), axis=0, tiled=True),
        )
        permuted = order[micro_step]
        dealt_tokens, dealt_cots = (
            lax.all_to_all(
                jnp.take(tokens[micro_step], permuted, axis=1),
                ("fsdp", "pair"),
                split_axis=1,
                concat_axis=0,
                tiled=True,
            ),
            lax.all_to_all(
                jnp.take(cotangent[micro_step], permuted, axis=1),
                ("fsdp", "pair"),
                split_axis=1,
                concat_axis=0,
                tiled=True,
            ),
        )
        length = lengths[micro_step][device_index]
        result, saved = forward_one(dealt_tokens[:, 0, :], dealt_cots[:, 0, :], length, weights)
        arrived = lax.all_to_all(
            result.astype(jnp.bfloat16)[:, None, :],
            ("fsdp", "pair"),
            split_axis=0,
            concat_axis=1,
            tiled=True,
        )
        outputs.append(restore(arrived, permuted))
        stored.append(saved)
    input_grads = [None] * batches
    records = [None] * batches
    gain_totals = None
    for micro_step in reversed(range(batches)):
        weights = fetch_backward(owned)
        d_start, record_rows, gain_sums = backward_one(stored[micro_step], weights)
        stored[micro_step] = None
        arrived = lax.all_to_all(
            d_start[:, None, :], ("fsdp", "pair"), split_axis=0, concat_axis=1, tiled=True
        )
        input_grads[micro_step] = restore(arrived, order[micro_step])
        records[micro_step] = record_rows
        gain_totals = gain_sums if gain_totals is None else add_tuples(gain_totals, gain_sums)
    joined = tuple(
        (
            jnp.concatenate([records[step][index] for step in range(batches)], 0)
            for index in range(11)
        )
    )
    hidden1, d_query, d_keys, d_values, attended, d_branch, hidden2, d_gate, d_up, inner, d_out = (
        joined
    )
    gain_cols = jnp.stack([gain_totals[0], gain_totals[1]], 1)
    g_query, g_key, g_value, g_out, g_gains = owner_sums(
        (
            take_rows(hidden1, d_query),
            take_rows(hidden1, d_keys),
            take_rows(hidden1, d_values),
            take_rows(attended, d_branch),
            gain_cols,
        )
    )
    g_gate, g_up = owner_sums((take_rows(hidden2, d_gate), take_rows(hidden2, d_up)))
    (g_down,) = owner_sums((take_rows(inner, d_out),))
    return (
        jnp.stack(outputs),
        jnp.stack(input_grads),
        g_gains[:, 0],
        g_query,
        g_key,
        g_value,
        g_out,
        g_gains[:, 1],
        g_gate,
        g_up,
        g_down,
    )


GRID = ("z", "y", "core", "pair")
SWAP = ((0, 1), (1, 0))


def swap(value, axis):
    return lax.ppermute(value, axis, SWAP)


def from_above(value, hops, size):
    return lax.ppermute(value, "z", [((i + hops) % size, i) for i in range(size)])


def matmul(left, right):
    return jnp.dot(left, right, preferred_element_type=jnp.float32)


def place_kernel(depth, *refs):
    blocks, whole, held, sems = refs[: 2 * depth], *refs[2 * depth :]
    z, y = lax.axis_index("z"), lax.axis_index("y")
    fetched, placed = [], []
    for side in range(2):
        for hops in range(depth):
            at = lax.rem(z + hops, depth) * 2 + (y if side == 0 else 1 - y)
            slot = side * depth + hops
            fetched.append(
                pltpu.make_async_copy(blocks[slot], held.at[slot], sems.at[0, slot])
            )
            placed.append(
                pltpu.make_async_copy(held.at[slot], whole.at[at], sems.at[1, slot])
            )
    for copy in fetched:
        copy.start()
    for arrived, copy in zip(fetched, placed):
        arrived.wait()
        copy.start()
    for copy in placed:
        copy.wait()


def place_blocks(blocks):
    depth = len(blocks) // 2
    shape, dtype = blocks[0].shape, blocks[0].dtype
    moved = 4 * depth * math.prod(shape) * dtype.itemsize
    return pl.pallas_call(
        functools.partial(place_kernel, depth),
        out_shape=jax.ShapeDtypeStruct((2 * depth,) + shape, dtype),
        in_specs=[pl.BlockSpec(memory_space=pl.ANY)] * (2 * depth),
        out_specs=pl.BlockSpec(memory_space=pl.ANY),
        scratch_shapes=[
            pltpu.VMEM((2 * depth,) + shape, dtype),
            pltpu.SemaphoreType.DMA((2, 2 * depth)),
        ],
        cost_estimate=pl.CostEstimate(flops=0, bytes_accessed=moved, transcendentals=0),
        name="place_blocks",
    )(*blocks)


def gather_zy(block, depth):
    column = [block] + [from_above(block, hops, depth) for hops in range(1, depth)]
    return place_blocks(column + [swap(part, "y") for part in column])


def reduce_z(partial, depth):
    z = lax.axis_index("z")
    total = lax.dynamic_index_in_dim(partial, z, 0, False).astype(jnp.float32)
    for hops in range(1, depth):
        sent = lax.dynamic_index_in_dim(
            partial, lax.rem(z + depth - hops, depth), 0, False
        )
        total = total + from_above(sent, hops, depth).astype(jnp.float32)
    return total


def halves(value, index, axis):
    return (
        lax.dynamic_index_in_dim(value, index, axis, False),
        lax.dynamic_index_in_dim(value, 1 - index, axis, False),
    )


def exchange_sum(value, index, axis, name):
    kept, sent = halves(value, index, axis)
    return (kept.astype(jnp.float32) + swap(sent, name).astype(jnp.float32)).astype(
        jnp.bfloat16
    )


def row_norm(value):
    return lax.rsqrt(jnp.mean(value * value, -1, keepdims=True) + EPSILON)


def norm_back(d_hidden, normed, scale, gain):
    d_norm = d_hidden * gain
    return scale * (d_norm - normed * jnp.mean(d_norm * normed, -1, keepdims=True))


def scores_of(query, keys, lens):
    seq_len = query.shape[1]
    features = query.shape[-1]
    scores = jnp.einsum(
        "bihe,bjhe->bhij", query, keys, preferred_element_type=jnp.float32
    ) * features ** (-0.5)
    row_ids = lax.broadcasted_iota(jnp.int32, (seq_len, seq_len), 0)
    col_ids = lax.broadcasted_iota(jnp.int32, (seq_len, seq_len), 1)
    mask = (col_ids <= row_ids)[None] & (col_ids[None] < lens[:, None, None])
    mask = mask[:, None]
    kernel = jnp.where(mask, 1.0 + scores + 0.5 * scores * scores, 0.0)
    denom = jnp.sum(kernel, -1, keepdims=True)
    return scores, mask, kernel / denom, denom


def attend(query, keys, values, lens):
    _, _, probs, _ = scores_of(query, keys, lens)
    return jnp.einsum(
        "bhij,bjhe->bihe", probs.astype(jnp.bfloat16), values, preferred_element_type=jnp.float32
    ).astype(jnp.bfloat16)


def attend_back(query, keys, values, lens, grads):
    scores, mask, probs, denom = scores_of(query, keys, lens)
    d_probs = jnp.einsum("bihe,bjhe->bhij", grads, values, preferred_element_type=jnp.float32)
    d_values = jnp.einsum(
        "bhij,bihe->bjhe", probs.astype(jnp.bfloat16), grads, preferred_element_type=jnp.float32
    )
    d_kernel = (d_probs - jnp.sum(d_probs * probs, -1, keepdims=True)) / denom
    d_scores = jnp.where(mask, d_kernel * (1.0 + scores), 0.0) * query.shape[-1] ** (-0.5)
    d_scores = d_scores.astype(jnp.bfloat16)
    d_query = jnp.einsum("bhij,bjhe->bihe", d_scores, keys, preferred_element_type=jnp.float32)
    d_keys = jnp.einsum("bhij,bihe->bjhe", d_scores, query, preferred_element_type=jnp.float32)
    return tuple(part.astype(jnp.bfloat16) for part in (d_query, d_keys, d_values))


def share_four(mine):
    near = swap(mine, "core")
    across = swap(mine, "pair")
    return jnp.concatenate([mine, near, across, swap(across, "core")], 0)


def sum_four(partial):
    count = partial.shape[0] // 4
    mine, near, across, far = (partial[i * count : (i + 1) * count] for i in range(4))
    got = swap(jnp.concatenate([near, far], 0).astype(jnp.bfloat16), "core").astype(jnp.float32)
    across = (across + got[count:]).astype(jnp.bfloat16)
    return mine + got[:count] + swap(across, "pair").astype(jnp.float32)


def on_grid(
    depth,
    tokens,
    cotangent,
    lengths,
    order,
    norm_gain,
    w_query,
    w_key,
    w_value,
    w_out,
    mlp_gain,
    w_gate,
    w_up,
    w_down,
):
    batches, _, seqs, width = tokens.shape
    core, pair = lax.axis_index("core"), lax.axis_index("pair")
    y = lax.axis_index("y")
    device_index = lax.axis_index(GRID)
    planes = 2 * depth
    rows_in = w_query.shape[0]
    ff_rows = w_down.shape[0]
    hidden = w_gate.shape[1]
    qk_width = w_query.shape[1]
    own_heads = HEADS // 2
    features = qk_width // HEADS
    head_dim = width // HEADS

    def core_columns(weight, step):
        return weight.reshape(rows_in, planes, 2, step)

    def half_heads(index):
        return jnp.concatenate(
            [
                lax.dynamic_index_in_dim(core_columns(weight, step), index, 2, False).reshape(rows_in, -1)
                for weight, step in ((w_query, features), (w_key, features), (w_value, head_dim))
            ],
            1,
        )

    qkv_mine = half_heads(core)
    qkv_got = swap(half_heads(1 - core), "core")
    qkv_block = jnp.where(
        core == 0, jnp.stack([qkv_mine, qkv_got]), jnp.stack([qkv_got, qkv_mine])
    ).reshape(2, rows_in, -1)
    w_qkv = gather_zy(qkv_block, depth)
    w_qkv_other = swap(w_qkv, "pair")
    w_qkv = jnp.where(
        pair == 0, jnp.stack([w_qkv, w_qkv_other], 2), jnp.stack([w_qkv_other, w_qkv], 2)
    ).reshape(width, -1)
    w_out_mine = gather_zy(w_out, depth)
    w_out_other = swap(w_out_mine, "pair")
    w_out_all = jnp.where(
        pair == 0, jnp.stack([w_out_mine, w_out_other], 1), jnp.stack([w_out_other, w_out_mine], 1)
    ).reshape(own_heads * head_dim, width)

    def hidden_block(weight):
        cut = weight.reshape(rows_in, planes, 2, 2, ff_rows)
        kept, sent = halves(cut, pair, 3)
        got = swap(sent.reshape(rows_in, -1), "pair").reshape(kept.shape)
        by_pair = jnp.where(pair == 0, jnp.stack([kept, got]), jnp.stack([got, kept]))
        kept, sent = halves(by_pair, core, 3)
        got = swap(sent.reshape(2, rows_in, -1), "core")
        kept = kept.reshape(got.shape)
        by_core = jnp.where(core == 0, jnp.stack([kept, got]), jnp.stack([got, kept]))
        return by_core.reshape(4 * rows_in, planes * ff_rows)

    w_gate_own = gather_zy(hidden_block(w_gate), depth).reshape(width, -1)
    w_up_own = gather_zy(hidden_block(w_up), depth).reshape(width, -1)
    w_down_own = gather_zy(w_down, depth).reshape(-1, width)

    gains = jnp.stack([norm_gain, mlp_gain])
    gains = lax.all_to_all(
        jnp.broadcast_to(gains[None], (seqs,) + gains.shape), GRID, split_axis=0, concat_axis=0, tiled=True
    )
    gains = gains.transpose(1, 0, 2).reshape(2, 1, width).astype(jnp.float32)
    gain1, gain2 = gains[0], gains[1]

    def deal(value):
        dealt = lax.all_to_all(value, GRID, split_axis=2, concat_axis=1, tiled=True)
        return dealt.reshape(-1, width)

    def undeal(value):
        return lax.all_to_all(
            value.reshape(batches, -1, 1, width), GRID, split_axis=1, concat_axis=2, tiled=True
        )

    start_rows = deal(tokens)
    cot_rows = deal(cotangent)
    count = start_rows.shape[0]
    seq_len = count // batches

    def lens_of(device):
        return jnp.sum(jnp.where(order == device, lengths, 0), 1)

    lens = jnp.concatenate([lens_of(device_index), lens_of(device_index + 2 - 4 * core)])
    live = (
        lax.broadcasted_iota(jnp.int32, (batches, seq_len), 1) < lens[:batches, None]
    ).reshape(count, 1)
    d_out = jnp.where(live, cot_rows, jnp.zeros_like(cot_rows))
    d_out_four = share_four(d_out)

    start = start_rows.astype(jnp.float32)
    scale1 = row_norm(start)
    hidden1 = (start * scale1 * gain1).astype(jnp.bfloat16)
    hidden1 = jnp.concatenate([hidden1, swap(hidden1, "core")], 0)
    qkv = matmul(hidden1, w_qkv).astype(jnp.bfloat16)
    own_qk = own_heads * features
    by_seq = (2 * batches, seq_len, own_heads, -1)
    query = qkv[:, :own_qk].reshape(by_seq)
    keys = qkv[:, own_qk : 2 * own_qk].reshape(by_seq)
    values = qkv[:, 2 * own_qk :].reshape(by_seq)
    attended = attend(query, keys, values, lens).reshape(2 * count, -1)
    branch = matmul(attended, w_out_all)
    resid = start + branch[:count] + swap(branch[count:], "core")
    scale2 = row_norm(resid)
    normed2 = resid * scale2
    hidden2 = share_four((normed2 * gain2).astype(jnp.bfloat16))

    gate_pre = matmul(hidden2, w_gate_own)
    up_pre = matmul(hidden2, w_up_own)
    sigma = jax.nn.sigmoid(gate_pre)
    inner = (gate_pre * sigma * up_pre).astype(jnp.bfloat16)
    result = resid + sum_four(matmul(inner, w_down_own))
    activations = undeal(result.astype(jnp.bfloat16))

    def owned_rows(partial):
        return reduce_z(exchange_sum(partial, y, 1, "y"), depth)

    def grid_rows(value):
        return value.reshape((depth, 2, -1) + value.shape[1:])

    g_down = owned_rows(grid_rows(take_rows(inner, d_out_four).astype(jnp.bfloat16)))

    d_inner = back_cols(d_out_four, w_down_own)
    d_gate = (d_inner * up_pre * sigma * (1.0 + gate_pre * (1.0 - sigma))).astype(jnp.bfloat16)
    d_up = (d_inner * gate_pre * sigma).astype(jnp.bfloat16)

    def owned_hidden(partial):
        rows = owned_rows(grid_rows(partial)).astype(jnp.bfloat16).reshape(2, 2, rows_in, -1)
        kept, sent = halves(rows, core, 0)
        got = swap(sent, "core")
        rows = jnp.where(core == 0, jnp.stack([kept, got]), jnp.stack([got, kept]))
        kept, sent = halves(rows, pair, 1)
        got = swap(sent, "pair")
        rows = jnp.where(pair == 0, jnp.stack([kept, got], 1), jnp.stack([got, kept], 1))
        rows = rows.reshape(2, 2, rows_in, planes, ff_rows).transpose(2, 3, 0, 1, 4)
        return rows.reshape(rows_in, hidden).astype(jnp.float32)

    g_gate = owned_hidden(take_rows(hidden2, d_gate).astype(jnp.bfloat16))
    g_up = owned_hidden(take_rows(hidden2, d_up).astype(jnp.bfloat16))

    d_hidden2 = sum_four(back_cols(d_gate, w_gate_own) + back_cols(d_up, w_up_own))
    g_mlp = jnp.sum(d_hidden2 * normed2, 0)
    d_resid = d_out.astype(jnp.float32) + norm_back(d_hidden2, normed2, scale2, gain2)
    d_branch = d_resid.astype(jnp.bfloat16)
    d_branch = jnp.concatenate([d_branch, swap(d_branch, "core")], 0)
    d_attended = back_cols(d_branch, w_out_all).astype(jnp.bfloat16)

    g_out = take_rows(attended, d_branch).astype(jnp.bfloat16)
    g_out = exchange_sum(g_out.reshape(planes, 2, rows_in, width), pair, 1, "pair")
    g_out = owned_rows(grid_rows(g_out.reshape(-1, width)))

    d_query, d_keys, d_values = attend_back(query, keys, values, lens, d_attended.reshape(by_seq))
    d_qkv = jnp.concatenate(
        [part.reshape(2 * count, -1) for part in (d_query, d_keys, d_values)], 1
    )
    d_hidden1 = back_cols(d_qkv, w_qkv)
    d_hidden1 = d_hidden1[:count] + swap(d_hidden1[count:], "core")
    normed1 = start * scale1
    g_norm = jnp.sum(d_hidden1 * normed1, 0)
    d_start = d_resid + norm_back(d_hidden1, normed1, scale1, gain1)
    input_grad = undeal(d_start.astype(jnp.bfloat16))

    g_qkv = take_rows(hidden1, d_qkv).astype(jnp.bfloat16)
    g_qkv = exchange_sum(g_qkv.reshape(planes, 2, 2, rows_in, -1), pair, 2, "pair")
    g_qkv = owned_rows(grid_rows(g_qkv.reshape(planes * 2 * rows_in, -1)))
    kept, sent = halves(g_qkv.astype(jnp.bfloat16).reshape(2, rows_in, -1), core, 0)
    got = swap(sent, "core")
    g_qkv = jnp.where(core == 0, jnp.stack([kept, got]), jnp.stack([got, kept]))

    def both_cores(part, step):
        part = part.reshape(2, rows_in, planes, step).transpose(1, 2, 0, 3)
        return part.reshape(rows_in, -1).astype(jnp.float32)

    g_query = both_cores(g_qkv[..., :own_qk], features)
    g_key = both_cores(g_qkv[..., own_qk : 2 * own_qk], features)
    g_value = both_cores(g_qkv[..., 2 * own_qk :], head_dim)

    g_gains = jnp.stack([g_norm, g_mlp]).reshape(2, seqs, rows_in).transpose(1, 0, 2)
    g_gains = jnp.sum(
        lax.all_to_all(g_gains, GRID, split_axis=0, concat_axis=0, tiled=True), 0
    )
    return (
        activations,
        input_grad,
        g_gains[0],
        g_query,
        g_key,
        g_value,
        g_out,
        g_gains[1],
        g_gate,
        g_up,
        g_down,
    )


def solution(mesh):
    fsdp, pair = mesh.shape["fsdp"], mesh.shape["pair"]
    names = ("fsdp", "pair")
    run = on_device
    if pair == 2 and fsdp == HEADS:
        names = GRID
        mesh = Mesh(mesh.devices.reshape(fsdp // 4, 2, 2, 2), GRID)
        run = functools.partial(on_grid, fsdp // 4)
    positions = P(None, names, None, None)
    rows, flat = P(names, None), P(names)
    return jax.shard_map(
        run,
        mesh=mesh,
        in_specs=(positions, positions, P(), P(), flat, rows, rows, rows, rows, flat, rows, rows, rows),
        out_specs=(positions, positions, flat, rows, rows, rows, rows, flat, rows, rows, rows),
        check_vma=False,
    )
```

```python
import functools
import math

import jax
import jax.numpy as jnp
from jax import lax
from jax.experimental import pallas as pl
from jax.experimental.pallas import tpu as pltpu
from jax.sharding import Mesh
from jax.sharding import PartitionSpec as P

HEADS = 16


PRECISE = lax.Precision.HIGHEST
EPSILON = 1e-06


def for_sending(shard):

    def short(part):
        return part.astype(jnp.bfloat16) if part.dtype == jnp.float32 else part

    return jax.tree.map(short, shard)


def take_rows(left, right):
    return lax.dot_general(
        left, right, (((0,), (0,)), ((), ())), preferred_element_type=jnp.float32
    )


def back_cols(left, right):
    return lax.dot_general(
        left, right, (((1,), (1,)), ((), ())), preferred_element_type=jnp.float32
    )


def kernel_terms(query, keys, length):
    seq_len = query.shape[0]
    features = query.shape[1] // HEADS
    query_heads = query.reshape(seq_len, HEADS, features)
    key_heads = keys.reshape(seq_len, HEADS, features)
    scores = jnp.einsum(
        "ihe,jhe->hij", query_heads, key_heads, preferred_element_type=jnp.float32
    ) * features ** (-0.5)
    row_ids = lax.broadcasted_iota(jnp.int32, (seq_len, seq_len), 0)
    col_ids = lax.broadcasted_iota(jnp.int32, (seq_len, seq_len), 1)
    key_mask = (col_ids <= row_ids) & (col_ids < length)
    kernel = jnp.where(key_mask[None], 1.0 + scores + 0.5 * scores * scores, 0.0)
    return (kernel, key_mask, scores)


def forward_one(start_rows, cot_rows, length, weights):
    norm_gain, w_query, w_key, w_value, w_out, mlp_gain, w_gate, w_up, w_down = weights
    seq_len, model_width = start_rows.shape
    start = start_rows.astype(jnp.float32)
    scale1 = lax.rsqrt(jnp.mean(start * start, -1, keepdims=True) + EPSILON)
    normed1 = start * scale1
    hidden1 = (normed1 * norm_gain.astype(jnp.float32)).astype(jnp.bfloat16)
    query = jnp.dot(hidden1, w_query, preferred_element_type=jnp.float32).astype(jnp.bfloat16)
    keys = jnp.dot(hidden1, w_key, preferred_element_type=jnp.float32).astype(jnp.bfloat16)
    values = jnp.dot(hidden1, w_value, preferred_element_type=jnp.float32).astype(jnp.bfloat16)
    kernel, key_mask, scores = kernel_terms(query, keys, length)
    denom = jnp.sum(kernel, -1)
    probs = (kernel / denom[..., None]).astype(jnp.bfloat16)
    value_heads = values.reshape(seq_len, HEADS, model_width // HEADS)
    mixed = jnp.einsum("hij,jhe->ihe", probs, value_heads, preferred_element_type=jnp.float32)
    attended = mixed.reshape(seq_len, model_width).astype(jnp.bfloat16)
    resid = start + jnp.dot(attended, w_out, preferred_element_type=jnp.float32)
    scale2 = lax.rsqrt(jnp.mean(resid * resid, -1, keepdims=True) + EPSILON)
    normed2 = resid * scale2
    hidden2 = (normed2 * mlp_gain.astype(jnp.float32)).astype(jnp.bfloat16)
    gate_pre = jnp.dot(hidden2, w_gate, preferred_element_type=jnp.float32)
    up_pre = jnp.dot(hidden2, w_up, preferred_element_type=jnp.float32)
    inner = (gate_pre * jax.nn.sigmoid(gate_pre) * up_pre).astype(jnp.bfloat16)
    result = resid + jnp.dot(inner, w_down, preferred_element_type=jnp.float32)
    saved = (
        cot_rows,
        length,
        normed1,
        scale1,
        hidden1,
        query,
        keys,
        values,
        denom,
        attended,
        normed2,
        scale2,
        hidden2,
        gate_pre,
        up_pre,
        inner,
    )
    return (result, saved)


def backward_one(saved, weights):
    norm_gain, w_query, w_key, w_value, w_out, mlp_gain, w_gate, w_up, w_down = weights
    (
        cot_rows,
        length,
        normed1,
        scale1,
        hidden1,
        query,
        keys,
        values,
        denom,
        attended,
        normed2,
        scale2,
        hidden2,
        gate_pre,
        up_pre,
        inner,
    ) = saved
    seq_len, model_width = normed1.shape
    live_rows = lax.broadcasted_iota(jnp.int32, (seq_len, 1), 0) < length
    d_out = jnp.where(live_rows, cot_rows, jnp.zeros_like(cot_rows))
    d_inner = back_cols(d_out, w_down)
    sigma = jax.nn.sigmoid(gate_pre)
    d_gate = (d_inner * up_pre * sigma * (1.0 + gate_pre * (1.0 - sigma))).astype(jnp.bfloat16)
    d_up = (d_inner * gate_pre * sigma).astype(jnp.bfloat16)
    d_hidden2 = back_cols(d_gate, w_gate) + back_cols(d_up, w_up)
    g_mlp = jnp.sum(d_hidden2 * normed2, 0)
    d_norm2 = d_hidden2 * mlp_gain.astype(jnp.float32)
    d_resid = d_out.astype(jnp.float32) + scale2 * (
        d_norm2 - normed2 * jnp.mean(d_norm2 * normed2, -1, keepdims=True)
    )
    d_branch = d_resid.astype(jnp.bfloat16)
    d_attended = back_cols(d_branch, w_out).astype(jnp.bfloat16)
    kernel, key_mask, scores = kernel_terms(query, keys, length)
    probs = kernel / denom[..., None]
    value_heads = values.reshape(seq_len, HEADS, model_width // HEADS)
    grad_heads = d_attended.reshape(seq_len, HEADS, model_width // HEADS)
    d_probs = jnp.einsum(
        "ihe,jhe->hij", grad_heads, value_heads, preferred_element_type=jnp.float32
    )
    d_values = jnp.einsum(
        "hij,ihe->jhe", probs.astype(jnp.bfloat16), grad_heads, preferred_element_type=jnp.float32
    )
    d_values = d_values.reshape(seq_len, model_width).astype(jnp.bfloat16)
    d_kernel = (d_probs - jnp.sum(d_probs * probs, -1, keepdims=True)) / denom[..., None]
    features = query.shape[1] // HEADS
    d_scores = jnp.where(key_mask[None], d_kernel * (1.0 + scores), 0.0) * features ** (-0.5)
    query_heads = query.reshape(seq_len, HEADS, features).astype(jnp.float32)
    key_heads = keys.reshape(seq_len, HEADS, features).astype(jnp.float32)
    d_query = (
        jnp.einsum("hij,jhe->ihe", d_scores, key_heads, precision=PRECISE)
        .reshape(seq_len, -1)
        .astype(jnp.bfloat16)
    )
    d_keys = (
        jnp.einsum("hij,ihe->jhe", d_scores, query_heads, precision=PRECISE)
        .reshape(seq_len, -1)
        .astype(jnp.bfloat16)
    )
    d_hidden1 = (
        back_cols(d_query, w_query) + back_cols(d_keys, w_key) + back_cols(d_values, w_value)
    )
    g_norm = jnp.sum(d_hidden1 * normed1, 0)
    d_norm1 = d_hidden1 * norm_gain.astype(jnp.float32)
    d_start = d_resid + scale1 * (
        d_norm1 - normed1 * jnp.mean(d_norm1 * normed1, -1, keepdims=True)
    )
    record_rows = (
        hidden1,
        d_query,
        d_keys,
        d_values,
        attended,
        d_branch,
        hidden2,
        d_gate,
        d_up,
        inner,
        d_out,
    )
    return (d_start.astype(jnp.bfloat16), record_rows, (g_norm, g_mlp))


def owner_sums(terms):
    arrived = jax.tree.map(
        lambda part, own: part.astype(own.dtype),
        lax.all_to_all(
            for_sending(terms), ("fsdp", "pair"), split_axis=0, concat_axis=0, tiled=True
        ),
        terms,
    )
    count = lax.axis_size(("fsdp", "pair"))
    return tuple(
        (
            jnp.sum(piece.reshape(count, piece.shape[0] // count, piece.shape[1]), 0)
            for piece in arrived
        )
    )


def restore(arrived, permuted):
    inverse = (
        jnp.zeros_like(permuted).at[permuted].set(jnp.arange(permuted.shape[0], dtype=jnp.int32))
    )
    return jnp.take(arrived, inverse, axis=1)


def fetch_backward(owned):
    return (
        lax.all_gather(owned[0], ("fsdp", "pair"), axis=0, tiled=True),
        lax.all_gather(owned[1], ("fsdp", "pair"), axis=0, tiled=True),
        lax.all_gather(owned[2], ("fsdp", "pair"), axis=0, tiled=True),
        lax.all_gather(owned[3], ("fsdp", "pair"), axis=0, tiled=True),
        lax.all_gather(owned[4], ("fsdp", "pair"), axis=0, tiled=True),
        lax.all_gather(owned[5], ("fsdp", "pair"), axis=0, tiled=True),
        lax.all_gather(owned[6], ("fsdp", "pair"), axis=0, tiled=True),
        lax.all_gather(owned[7], ("fsdp", "pair"), axis=0, tiled=True),
        lax.all_gather(owned[8], ("fsdp", "pair"), axis=0, tiled=True),
    )


def add_tuples(first_tuple, second_tuple):
    return tuple((first + second for first, second in zip(first_tuple, second_tuple)))


def on_device(
    tokens,
    cotangent,
    lengths,
    order,
    norm_gain,
    w_query,
    w_key,
    w_value,
    w_out,
    mlp_gain,
    w_gate,
    w_up,
    w_down,
):
    owned = (norm_gain, w_query, w_key, w_value, w_out, mlp_gain, w_gate, w_up, w_down)
    batches = tokens.shape[0]
    device_index = lax.axis_index(("fsdp", "pair"))
    stored = []
    outputs = []
    for micro_step in range(batches):
        weights = (
            lax.all_gather(owned[0], ("fsdp", "pair"), axis=0, tiled=True),
            lax.all_gather(owned[1], ("fsdp", "pair"), axis=0, tiled=True),
            lax.all_gather(owned[2], ("fsdp", "pair"), axis=0, tiled=True),
            lax.all_gather(owned[3], ("fsdp", "pair"), axis=0, tiled=True),
            lax.all_gather(owned[4], ("fsdp", "pair"), axis=0, tiled=True),
            lax.all_gather(owned[5], ("fsdp", "pair"), axis=0, tiled=True),
            lax.all_gather(owned[6], ("fsdp", "pair"), axis=0, tiled=True),
            lax.all_gather(owned[7], ("fsdp", "pair"), axis=0, tiled=True),
            lax.all_gather(owned[8], ("fsdp", "pair"), axis=0, tiled=True),
        )
        permuted = order[micro_step]
        dealt_tokens, dealt_cots = (
            lax.all_to_all(
                jnp.take(tokens[micro_step], permuted, axis=1),
                ("fsdp", "pair"),
                split_axis=1,
                concat_axis=0,
                tiled=True,
            ),
            lax.all_to_all(
                jnp.take(cotangent[micro_step], permuted, axis=1),
                ("fsdp", "pair"),
                split_axis=1,
                concat_axis=0,
                tiled=True,
            ),
        )
        length = lengths[micro_step][device_index]
        result, saved = forward_one(dealt_tokens[:, 0, :], dealt_cots[:, 0, :], length, weights)
        arrived = lax.all_to_all(
            result.astype(jnp.bfloat16)[:, None, :],
            ("fsdp", "pair"),
            split_axis=0,
            concat_axis=1,
            tiled=True,
        )
        outputs.append(restore(arrived, permuted))
        stored.append(saved)
    input_grads = [None] * batches
    records = [None] * batches
    gain_totals = None
    for micro_step in reversed(range(batches)):
        weights = fetch_backward(owned)
        d_start, record_rows, gain_sums = backward_one(stored[micro_step], weights)
        stored[micro_step] = None
        arrived = lax.all_to_all(
            d_start[:, None, :], ("fsdp", "pair"), split_axis=0, concat_axis=1, tiled=True
        )
        input_grads[micro_step] = restore(arrived, order[micro_step])
        records[micro_step] = record_rows
        gain_totals = gain_sums if gain_totals is None else add_tuples(gain_totals, gain_sums)
    joined = tuple(
        (
            jnp.concatenate([records[step][index] for step in range(batches)], 0)
            for index in range(11)
        )
    )
    hidden1, d_query, d_keys, d_values, attended, d_branch, hidden2, d_gate, d_up, inner, d_out = (
        joined
    )
    gain_cols = jnp.stack([gain_totals[0], gain_totals[1]], 1)
    g_query, g_key, g_value, g_out, g_gains = owner_sums(
        (
            take_rows(hidden1, d_query),
            take_rows(hidden1, d_keys),
            take_rows(hidden1, d_values),
            take_rows(attended, d_branch),
            gain_cols,
        )
    )
    g_gate, g_up = owner_sums((take_rows(hidden2, d_gate), take_rows(hidden2, d_up)))
    (g_down,) = owner_sums((take_rows(inner, d_out),))
    return (
        jnp.stack(outputs),
        jnp.stack(input_grads),
        g_gains[:, 0],
        g_query,
        g_key,
        g_value,
        g_out,
        g_gains[:, 1],
        g_gate,
        g_up,
        g_down,
    )


GRID = ("z", "y", "core", "pair")
SWAP = ((0, 1), (1, 0))
LANES = 128


def swap(value, axis):
    return lax.ppermute(value, axis, SWAP)


def from_above(value, hops, size):
    return lax.ppermute(value, "z", [((i + hops) % size, i) for i in range(size)])


def after(value, *earlier):
    return lax.optimization_barrier((value, *earlier))[0]


def short(value):
    return value.astype(jnp.bfloat16)


def long(value):
    return value.astype(jnp.float32)


def matmul(left, right):
    return jnp.dot(left, right, preferred_element_type=jnp.float32)


def place_kernel(depth, *refs):
    blocks, whole, held, sems = refs[:depth], *refs[depth:]
    z = lax.axis_index("z")
    fetched, placed = [], []
    for hops in range(depth):
        at = lax.rem(z + hops, depth)
        fetched.append(
            pltpu.make_async_copy(blocks[hops], held.at[hops], sems.at[0, hops])
        )
        placed.append(
            pltpu.make_async_copy(held.at[hops], whole.at[at], sems.at[1, hops])
        )
    for copy in fetched:
        copy.start()
    for arrived, copy in zip(fetched, placed):
        arrived.wait()
        copy.start()
    for copy in placed:
        copy.wait()


def place_blocks(blocks):
    depth = len(blocks)
    shape, dtype = blocks[0].shape, blocks[0].dtype
    moved = 2 * depth * math.prod(shape) * dtype.itemsize
    return pl.pallas_call(
        functools.partial(place_kernel, depth),
        out_shape=jax.ShapeDtypeStruct((depth,) + shape, dtype),
        in_specs=[pl.BlockSpec(memory_space=pl.ANY)] * depth,
        out_specs=pl.BlockSpec(memory_space=pl.ANY),
        scratch_shapes=[
            pltpu.VMEM((depth,) + shape, dtype),
            pltpu.SemaphoreType.DMA((2, depth)),
        ],
        cost_estimate=pl.CostEstimate(flops=0, bytes_accessed=moved, transcendentals=0),
        name="place_blocks",
    )(*blocks)


def column_of(block, depth):
    return [block] + [from_above(block, hops, depth) for hops in range(1, depth)]


def gather_z(block):
    return lax.all_gather(block, "z", axis=0, tiled=True)


def scatter_z(partial):
    return lax.psum_scatter(partial, "z", scatter_dimension=0, tiled=True)


def reduce_z(partial, depth):
    z = lax.axis_index("z")
    total = long(lax.dynamic_index_in_dim(partial, z, 0, False))
    for hops in range(1, depth):
        sent = lax.dynamic_index_in_dim(
            partial, lax.rem(z + depth - hops, depth), 0, False
        )
        total = total + long(from_above(sent, hops, depth))
    return total


def halves(value, index, axis):
    return (
        lax.dynamic_index_in_dim(value, index, axis, False),
        lax.dynamic_index_in_dim(value, 1 - index, axis, False),
    )


def both(mine, other, index, axis):
    return jnp.where(
        index == 0, jnp.stack([mine, other], axis), jnp.stack([other, mine], axis)
    )


def trade(value, name, axis, into):
    index = lax.axis_index(name)
    kept, sent = halves(value, index, axis)
    flat = sent.reshape(-1, sent.shape[-1]) if sent.ndim > 2 else sent
    return both(kept, swap(flat, name).reshape(kept.shape), index, into)


def row_norm(value):
    return lax.rsqrt(jnp.mean(value * value, -1, keepdims=True) + EPSILON)


def norm_back(d_hidden, normed, scale, gain):
    d_norm = d_hidden * gain
    return scale * (d_norm - normed * jnp.mean(d_norm * normed, -1, keepdims=True))


def scores_of(query, keys, lens):
    seq_len = query.shape[1]
    features = query.shape[-1]
    scores = jnp.einsum(
        "bihe,bjhe->bhij", query, keys, preferred_element_type=jnp.float32
    ) * features ** (-0.5)
    row_ids = lax.broadcasted_iota(jnp.int32, (seq_len, seq_len), 0)
    col_ids = lax.broadcasted_iota(jnp.int32, (seq_len, seq_len), 1)
    mask = (col_ids <= row_ids)[None] & (col_ids[None] < lens[:, None, None])
    mask = mask[:, None]
    kernel = jnp.where(mask, 1.0 + scores + 0.5 * scores * scores, 0.0)
    denom = jnp.sum(kernel, -1, keepdims=True)
    return scores, mask, kernel / denom, denom


def attend(query, keys, values, lens):
    _, _, probs, _ = scores_of(query, keys, lens)
    return short(
        jnp.einsum("bhij,bjhe->bihe", short(probs), values, preferred_element_type=jnp.float32)
    )


def attend_back(query, keys, values, lens, grads):
    scores, mask, probs, denom = scores_of(query, keys, lens)
    d_probs = jnp.einsum("bihe,bjhe->bhij", grads, values, preferred_element_type=jnp.float32)
    d_values = jnp.einsum(
        "bhij,bihe->bjhe", short(probs), grads, preferred_element_type=jnp.float32
    )
    d_kernel = (d_probs - jnp.sum(d_probs * probs, -1, keepdims=True)) / denom
    d_scores = jnp.where(mask, d_kernel * (1.0 + scores), 0.0) * query.shape[-1] ** (-0.5)
    d_scores = short(d_scores)
    d_query = jnp.einsum("bhij,bjhe->bihe", d_scores, keys, preferred_element_type=jnp.float32)
    d_keys = jnp.einsum("bhij,bihe->bjhe", d_scores, query, preferred_element_type=jnp.float32)
    return short(d_query), short(d_keys), short(d_values)


def share_four(mine):
    up = swap(mine, "y")
    return jnp.concatenate([mine, up, swap(mine, "core"), swap(up, "core")], 0)


def sum_four(partial):
    count = partial.shape[0] // 4
    got = swap(partial[2 * count :], "core")
    up = short(long(partial[count : 2 * count]) + long(got[count:]))
    return long(partial[:count]) + long(got[:count]) + long(swap(up, "y"))


def share_eight(mine):
    half = mine.shape[0] // 2
    up, across = swap(mine, "y"), swap(mine, "pair")
    far_a = swap(across[:half], "y")
    far_b = swap(up[half:], "pair")
    own = [mine, up, across, far_a, far_b]
    near = [swap(mine, "core"), swap(up, "core"), swap(across, "core")]
    near += [swap(far_a, "core"), swap(far_b, "core")]
    return jnp.concatenate(own + near, 0)


def sum_eight(partial):
    count = partial.shape[0] // 8
    half = count // 2
    got = swap(partial[4 * count :], "core")
    own = long(partial[: 4 * count]) + long(got)
    far = short(own[3 * count :])
    mine, up, across = (own[i * count : (i + 1) * count] for i in range(3))
    near_a, near_b = swap(far[:half], "y"), swap(far[half:], "pair")
    across = jnp.concatenate([across[:half] + long(near_a), across[half:]], 0)
    up = jnp.concatenate([up[:half], up[half:] + long(near_b)], 0)
    return mine + long(swap(short(up), "y")) + long(swap(short(across), "pair"))


def on_grid(
    depth,
    tokens,
    cotangent,
    lengths,
    order,
    norm_gain,
    w_query,
    w_key,
    w_value,
    w_out,
    mlp_gain,
    w_gate,
    w_up,
    w_down,
):
    batches, _, seqs, width = tokens.shape
    y, core, pair = (lax.axis_index(name) for name in ("y", "core", "pair"))
    device_index = lax.axis_index(GRID)
    rows_in, hidden = w_gate.shape
    ff_rows = w_down.shape[0]
    own_ff = depth * ff_rows
    wide = -(-own_ff // LANES) * LANES
    own_heads = depth
    features = w_query.shape[1] // HEADS
    head_dim = width // HEADS
    own_qk = own_heads * features

    def deal(value):
        dealt = lax.all_to_all(value, GRID, split_axis=2, concat_axis=1, tiled=True)
        return dealt.reshape(-1, width)

    def undeal(value):
        return lax.all_to_all(
            value.reshape(batches, -1, 1, width), GRID, split_axis=1, concat_axis=2, tiled=True
        )

    gains = jnp.stack([norm_gain, mlp_gain])
    gains = lax.all_to_all(
        jnp.broadcast_to(gains[None], (seqs,) + gains.shape), GRID, split_axis=0, concat_axis=0, tiled=True
    )
    gains = long(gains.transpose(1, 0, 2).reshape(2, 1, width))
    gain1, gain2 = gains[0], gains[1]
    start_rows = deal(tokens)

    qkv = jnp.concatenate(
        [
            weight.reshape(rows_in, depth, 2, 2, step).transpose(2, 3, 0, 1, 4).reshape(2, 2, rows_in, -1)
            for weight, step in ((w_query, features), (w_key, features), (w_value, head_dim))
        ],
        3,
    )
    qkv = trade(trade(qkv, "core", 1, 1), "y", 0, 0)
    out_column = column_of(w_out, depth)
    qkv_column = column_of(qkv.reshape(4 * rows_in, -1), depth)

    def joined(column, shape, axis):
        mine = place_blocks(column)
        return both(mine.reshape(shape), swap(mine, "pair").reshape(shape), pair, axis)

    w_qkv = joined(qkv_column, (4 * depth, rows_in, -1), 1).reshape(width, -1)
    w_out_own = joined(out_column, (depth, rows_in, width), 1).reshape(-1, width)

    def hidden_block(weight):
        cut = weight.reshape(rows_in, depth, 2, 2, 2, ff_rows)
        cut = cut.transpose(2, 3, 4, 0, 1, 5).reshape(2, 2, 2, rows_in, own_ff)
        return cut

    cut = jnp.concatenate([hidden_block(w_gate), hidden_block(w_up)], 4)
    cut = trade(cut, "y", 0, 0)
    cut = trade(cut, "pair", 2, 2)
    cut = trade(cut, "core", 1, 1).reshape(8 * rows_in, 2 * own_ff)
    gate_up = gather_z(cut)
    cot_rows = deal(after(cotangent, cut))
    filler = jnp.zeros((width, wide - own_ff), jnp.bfloat16)
    gate_up = jnp.concatenate([gate_up[:, :own_ff], filler, gate_up[:, own_ff:], filler], 1)
    w_down_own = jnp.pad(gather_z(w_down), ((0, wide - own_ff), (0, 0)))

    count = start_rows.shape[0]
    seq_len = count // batches

    def lens_of(device):
        return jnp.sum(jnp.where(order == device, lengths, 0), 1)

    by_core, by_y = device_index + 2 - 4 * core, 4 - 8 * y
    lens = jnp.concatenate(
        [lens_of(device_index), lens_of(device_index + by_y), lens_of(by_core), lens_of(by_core + by_y)]
    )
    live = (
        lax.broadcasted_iota(jnp.int32, (batches, seq_len), 1) < lens[:batches, None]
    ).reshape(count, 1)
    d_out = jnp.where(live, cot_rows, jnp.zeros_like(cot_rows))
    d_out_all = share_eight(d_out)

    start = long(start_rows)
    scale1 = row_norm(start)
    hidden1 = share_four(short(start * scale1 * gain1))
    qkv = short(matmul(hidden1, w_qkv))
    by_seq = (4 * batches, seq_len, own_heads, -1)
    query = qkv[:, :own_qk].reshape(by_seq)
    keys = qkv[:, own_qk : 2 * own_qk].reshape(by_seq)
    values = qkv[:, 2 * own_qk :].reshape(by_seq)
    attended = attend(query, keys, values, lens).reshape(4 * count, -1)
    resid = start + sum_four(short(matmul(attended, w_out_own)))
    scale2 = row_norm(resid)
    normed2 = resid * scale2
    hidden2 = share_eight(short(normed2 * gain2))

    both_pre = matmul(hidden2, gate_up)
    gate_pre, up_pre = both_pre[:, :wide], both_pre[:, wide:]
    sigma = jax.nn.sigmoid(gate_pre)
    inner = short(gate_pre * sigma * up_pre)
    g_down = short(take_rows(inner, d_out_all)[:own_ff])
    d_out_all, g_down = lax.optimization_barrier((d_out_all, g_down))
    g_down = long(scatter_z(g_down))

    d_inner = back_cols(d_out_all, w_down_own)
    d_gate = short(d_inner * up_pre * sigma * (1.0 + gate_pre * (1.0 - sigma)))
    d_up = short(d_inner * gate_pre * sigma)
    d_both = jnp.concatenate([d_gate, d_up], 1)

    def owned_hidden(columns):
        rows = jnp.concatenate([columns[:, :own_ff], columns[:, wide : wide + own_ff]], 1)
        rows = scatter_z(rows)
        rows = rows.reshape(2, 2, 2, rows_in, -1)
        rows = trade(rows, "y", 0, 0)
        rows = trade(rows, "pair", 2, 2)
        rows = trade(rows, "core", 1, 1)
        def natural(part):
            part = part.reshape(2, 2, 2, rows_in, depth, ff_rows).transpose(3, 4, 0, 1, 2, 5)
            return long(part.reshape(rows_in, hidden))
        return natural(rows[..., :own_ff]), natural(rows[..., own_ff:])

    g_both = short(take_rows(hidden2, d_both))
    d_both, inner, g_both = lax.optimization_barrier((d_both, inner, g_both))
    g_gate, g_up = owned_hidden(g_both)
    d_hidden2 = sum_eight(short(back_cols(d_both, gate_up)))
    result = resid + sum_eight(short(matmul(inner, w_down_own)))
    activations = undeal(short(result))

    g_mlp = jnp.sum(d_hidden2 * normed2, 0)
    d_resid = long(d_out) + norm_back(d_hidden2, normed2, scale2, gain2)
    d_branch = share_four(short(d_resid))
    d_attended = short(back_cols(d_branch, w_out_own))

    def owned_rows(partial):
        kept, sent = halves(partial, pair, 2)
        got = swap(sent.reshape(-1, sent.shape[-1]), "pair").reshape(kept.shape)
        rows = short(long(kept) + long(got))
        return reduce_z(rows.reshape(depth, -1, rows.shape[-1]), depth)

    g_out = short(take_rows(attended, d_branch))
    g_out = owned_rows(g_out.reshape(depth, 1, 2, rows_in, width))

    d_query, d_keys, d_values = attend_back(query, keys, values, lens, d_attended.reshape(by_seq))
    d_qkv = jnp.concatenate(
        [part.reshape(4 * count, -1) for part in (d_query, d_keys, d_values)], 1
    )
    g_qkv = short(take_rows(hidden1, d_qkv))
    g_qkv = short(owned_rows(g_qkv.reshape(depth, 4, 2, rows_in, -1)))
    g_qkv = trade(trade(g_qkv.reshape(2, 2, rows_in, -1), "y", 0, 0), "core", 1, 1)

    def all_heads(part, step):
        part = part.reshape(2, 2, rows_in, depth, step).transpose(2, 3, 0, 1, 4)
        return long(part.reshape(rows_in, -1))

    g_query = all_heads(g_qkv[..., :own_qk], features)
    g_key = all_heads(g_qkv[..., own_qk : 2 * own_qk], features)
    g_value = all_heads(g_qkv[..., 2 * own_qk :], head_dim)

    d_hidden1 = sum_four(short(back_cols(d_qkv, w_qkv)))
    normed1 = start * scale1
    g_norm = jnp.sum(d_hidden1 * normed1, 0)
    d_start = d_resid + norm_back(d_hidden1, normed1, scale1, gain1)
    input_grad = undeal(short(d_start))

    g_gains = jnp.stack([g_norm, g_mlp]).reshape(2, seqs, rows_in).transpose(1, 0, 2)
    g_gains = jnp.sum(
        lax.all_to_all(g_gains, GRID, split_axis=0, concat_axis=0, tiled=True), 0
    )
    return (
        activations,
        input_grad,
        g_gains[0],
        g_query,
        g_key,
        g_value,
        g_out,
        g_gains[1],
        g_gate,
        g_up,
        g_down,
    )


def solution(mesh):
    fsdp, pair = mesh.shape["fsdp"], mesh.shape["pair"]
    names = ("fsdp", "pair")
    run = on_device
    if pair == 2 and fsdp == HEADS:
        names = GRID
        mesh = Mesh(mesh.devices.reshape(fsdp // 4, 2, 2, 2), GRID)
        run = functools.partial(on_grid, fsdp // 4)
    positions = P(None, names, None, None)
    rows, flat = P(names, None), P(names)
    return jax.shard_map(
        run,
        mesh=mesh,
        in_specs=(positions, positions, P(), P(), flat, rows, rows, rows, rows, flat, rows, rows, rows),
        out_specs=(positions, positions, flat, rows, rows, rows, rows, flat, rows, rows, rows),
        check_vma=False,
    )
```

```python
import functools
import math

import jax
import jax.numpy as jnp
from jax import lax
from jax.experimental import pallas as pl
from jax.experimental.pallas import tpu as pltpu
from jax.sharding import Mesh
from jax.sharding import PartitionSpec as P

HEADS = 16


PRECISE = lax.Precision.HIGHEST
EPSILON = 1e-06


def for_sending(shard):

    def short(part):
        return part.astype(jnp.bfloat16) if part.dtype == jnp.float32 else part

    return jax.tree.map(short, shard)


def take_rows(left, right):
    return lax.dot_general(
        left, right, (((0,), (0,)), ((), ())), preferred_element_type=jnp.float32
    )


def back_cols(left, right):
    return lax.dot_general(
        left, right, (((1,), (1,)), ((), ())), preferred_element_type=jnp.float32
    )


def kernel_terms(query, keys, length):
    seq_len = query.shape[0]
    features = query.shape[1] // HEADS
    query_heads = query.reshape(seq_len, HEADS, features)
    key_heads = keys.reshape(seq_len, HEADS, features)
    scores = jnp.einsum(
        "ihe,jhe->hij", query_heads, key_heads, preferred_element_type=jnp.float32
    ) * features ** (-0.5)
    row_ids = lax.broadcasted_iota(jnp.int32, (seq_len, seq_len), 0)
    col_ids = lax.broadcasted_iota(jnp.int32, (seq_len, seq_len), 1)
    key_mask = (col_ids <= row_ids) & (col_ids < length)
    kernel = jnp.where(key_mask[None], 1.0 + scores + 0.5 * scores * scores, 0.0)
    return (kernel, key_mask, scores)


def forward_one(start_rows, cot_rows, length, weights):
    norm_gain, w_query, w_key, w_value, w_out, mlp_gain, w_gate, w_up, w_down = weights
    seq_len, model_width = start_rows.shape
    start = start_rows.astype(jnp.float32)
    scale1 = lax.rsqrt(jnp.mean(start * start, -1, keepdims=True) + EPSILON)
    normed1 = start * scale1
    hidden1 = (normed1 * norm_gain.astype(jnp.float32)).astype(jnp.bfloat16)
    query = jnp.dot(hidden1, w_query, preferred_element_type=jnp.float32).astype(jnp.bfloat16)
    keys = jnp.dot(hidden1, w_key, preferred_element_type=jnp.float32).astype(jnp.bfloat16)
    values = jnp.dot(hidden1, w_value, preferred_element_type=jnp.float32).astype(jnp.bfloat16)
    kernel, key_mask, scores = kernel_terms(query, keys, length)
    denom = jnp.sum(kernel, -1)
    probs = (kernel / denom[..., None]).astype(jnp.bfloat16)
    value_heads = values.reshape(seq_len, HEADS, model_width // HEADS)
    mixed = jnp.einsum("hij,jhe->ihe", probs, value_heads, preferred_element_type=jnp.float32)
    attended = mixed.reshape(seq_len, model_width).astype(jnp.bfloat16)
    resid = start + jnp.dot(attended, w_out, preferred_element_type=jnp.float32)
    scale2 = lax.rsqrt(jnp.mean(resid * resid, -1, keepdims=True) + EPSILON)
    normed2 = resid * scale2
    hidden2 = (normed2 * mlp_gain.astype(jnp.float32)).astype(jnp.bfloat16)
    gate_pre = jnp.dot(hidden2, w_gate, preferred_element_type=jnp.float32)
    up_pre = jnp.dot(hidden2, w_up, preferred_element_type=jnp.float32)
    inner = (gate_pre * jax.nn.sigmoid(gate_pre) * up_pre).astype(jnp.bfloat16)
    result = resid + jnp.dot(inner, w_down, preferred_element_type=jnp.float32)
    saved = (
        cot_rows,
        length,
        normed1,
        scale1,
        hidden1,
        query,
        keys,
        values,
        denom,
        attended,
        normed2,
        scale2,
        hidden2,
        gate_pre,
        up_pre,
        inner,
    )
    return (result, saved)


def backward_one(saved, weights):
    norm_gain, w_query, w_key, w_value, w_out, mlp_gain, w_gate, w_up, w_down = weights
    (
        cot_rows,
        length,
        normed1,
        scale1,
        hidden1,
        query,
        keys,
        values,
        denom,
        attended,
        normed2,
        scale2,
        hidden2,
        gate_pre,
        up_pre,
        inner,
    ) = saved
    seq_len, model_width = normed1.shape
    live_rows = lax.broadcasted_iota(jnp.int32, (seq_len, 1), 0) < length
    d_out = jnp.where(live_rows, cot_rows, jnp.zeros_like(cot_rows))
    d_inner = back_cols(d_out, w_down)
    sigma = jax.nn.sigmoid(gate_pre)
    d_gate = (d_inner * up_pre * sigma * (1.0 + gate_pre * (1.0 - sigma))).astype(jnp.bfloat16)
    d_up = (d_inner * gate_pre * sigma).astype(jnp.bfloat16)
    d_hidden2 = back_cols(d_gate, w_gate) + back_cols(d_up, w_up)
    g_mlp = jnp.sum(d_hidden2 * normed2, 0)
    d_norm2 = d_hidden2 * mlp_gain.astype(jnp.float32)
    d_resid = d_out.astype(jnp.float32) + scale2 * (
        d_norm2 - normed2 * jnp.mean(d_norm2 * normed2, -1, keepdims=True)
    )
    d_branch = d_resid.astype(jnp.bfloat16)
    d_attended = back_cols(d_branch, w_out).astype(jnp.bfloat16)
    kernel, key_mask, scores = kernel_terms(query, keys, length)
    probs = kernel / denom[..., None]
    value_heads = values.reshape(seq_len, HEADS, model_width // HEADS)
    grad_heads = d_attended.reshape(seq_len, HEADS, model_width // HEADS)
    d_probs = jnp.einsum(
        "ihe,jhe->hij", grad_heads, value_heads, preferred_element_type=jnp.float32
    )
    d_values = jnp.einsum(
        "hij,ihe->jhe", probs.astype(jnp.bfloat16), grad_heads, preferred_element_type=jnp.float32
    )
    d_values = d_values.reshape(seq_len, model_width).astype(jnp.bfloat16)
    d_kernel = (d_probs - jnp.sum(d_probs * probs, -1, keepdims=True)) / denom[..., None]
    features = query.shape[1] // HEADS
    d_scores = jnp.where(key_mask[None], d_kernel * (1.0 + scores), 0.0) * features ** (-0.5)
    query_heads = query.reshape(seq_len, HEADS, features).astype(jnp.float32)
    key_heads = keys.reshape(seq_len, HEADS, features).astype(jnp.float32)
    d_query = (
        jnp.einsum("hij,jhe->ihe", d_scores, key_heads, precision=PRECISE)
        .reshape(seq_len, -1)
        .astype(jnp.bfloat16)
    )
    d_keys = (
        jnp.einsum("hij,ihe->jhe", d_scores, query_heads, precision=PRECISE)
        .reshape(seq_len, -1)
        .astype(jnp.bfloat16)
    )
    d_hidden1 = (
        back_cols(d_query, w_query) + back_cols(d_keys, w_key) + back_cols(d_values, w_value)
    )
    g_norm = jnp.sum(d_hidden1 * normed1, 0)
    d_norm1 = d_hidden1 * norm_gain.astype(jnp.float32)
    d_start = d_resid + scale1 * (
        d_norm1 - normed1 * jnp.mean(d_norm1 * normed1, -1, keepdims=True)
    )
    record_rows = (
        hidden1,
        d_query,
        d_keys,
        d_values,
        attended,
        d_branch,
        hidden2,
        d_gate,
        d_up,
        inner,
        d_out,
    )
    return (d_start.astype(jnp.bfloat16), record_rows, (g_norm, g_mlp))


def owner_sums(terms):
    arrived = jax.tree.map(
        lambda part, own: part.astype(own.dtype),
        lax.all_to_all(
            for_sending(terms), ("fsdp", "pair"), split_axis=0, concat_axis=0, tiled=True
        ),
        terms,
    )
    count = lax.axis_size(("fsdp", "pair"))
    return tuple(
        (
            jnp.sum(piece.reshape(count, piece.shape[0] // count, piece.shape[1]), 0)
            for piece in arrived
        )
    )


def restore(arrived, permuted):
    inverse = (
        jnp.zeros_like(permuted).at[permuted].set(jnp.arange(permuted.shape[0], dtype=jnp.int32))
    )
    return jnp.take(arrived, inverse, axis=1)


def fetch_backward(owned):
    return (
        lax.all_gather(owned[0], ("fsdp", "pair"), axis=0, tiled=True),
        lax.all_gather(owned[1], ("fsdp", "pair"), axis=0, tiled=True),
        lax.all_gather(owned[2], ("fsdp", "pair"), axis=0, tiled=True),
        lax.all_gather(owned[3], ("fsdp", "pair"), axis=0, tiled=True),
        lax.all_gather(owned[4], ("fsdp", "pair"), axis=0, tiled=True),
        lax.all_gather(owned[5], ("fsdp", "pair"), axis=0, tiled=True),
        lax.all_gather(owned[6], ("fsdp", "pair"), axis=0, tiled=True),
        lax.all_gather(owned[7], ("fsdp", "pair"), axis=0, tiled=True),
        lax.all_gather(owned[8], ("fsdp", "pair"), axis=0, tiled=True),
    )


def add_tuples(first_tuple, second_tuple):
    return tuple((first + second for first, second in zip(first_tuple, second_tuple)))


def on_device(
    tokens,
    cotangent,
    lengths,
    order,
    norm_gain,
    w_query,
    w_key,
    w_value,
    w_out,
    mlp_gain,
    w_gate,
    w_up,
    w_down,
):
    owned = (norm_gain, w_query, w_key, w_value, w_out, mlp_gain, w_gate, w_up, w_down)
    batches = tokens.shape[0]
    device_index = lax.axis_index(("fsdp", "pair"))
    stored = []
    outputs = []
    for micro_step in range(batches):
        weights = (
            lax.all_gather(owned[0], ("fsdp", "pair"), axis=0, tiled=True),
            lax.all_gather(owned[1], ("fsdp", "pair"), axis=0, tiled=True),
            lax.all_gather(owned[2], ("fsdp", "pair"), axis=0, tiled=True),
            lax.all_gather(owned[3], ("fsdp", "pair"), axis=0, tiled=True),
            lax.all_gather(owned[4], ("fsdp", "pair"), axis=0, tiled=True),
            lax.all_gather(owned[5], ("fsdp", "pair"), axis=0, tiled=True),
            lax.all_gather(owned[6], ("fsdp", "pair"), axis=0, tiled=True),
            lax.all_gather(owned[7], ("fsdp", "pair"), axis=0, tiled=True),
            lax.all_gather(owned[8], ("fsdp", "pair"), axis=0, tiled=True),
        )
        permuted = order[micro_step]
        dealt_tokens, dealt_cots = (
            lax.all_to_all(
                jnp.take(tokens[micro_step], permuted, axis=1),
                ("fsdp", "pair"),
                split_axis=1,
                concat_axis=0,
                tiled=True,
            ),
            lax.all_to_all(
                jnp.take(cotangent[micro_step], permuted, axis=1),
                ("fsdp", "pair"),
                split_axis=1,
                concat_axis=0,
                tiled=True,
            ),
        )
        length = lengths[micro_step][device_index]
        result, saved = forward_one(dealt_tokens[:, 0, :], dealt_cots[:, 0, :], length, weights)
        arrived = lax.all_to_all(
            result.astype(jnp.bfloat16)[:, None, :],
            ("fsdp", "pair"),
            split_axis=0,
            concat_axis=1,
            tiled=True,
        )
        outputs.append(restore(arrived, permuted))
        stored.append(saved)
    input_grads = [None] * batches
    records = [None] * batches
    gain_totals = None
    for micro_step in reversed(range(batches)):
        weights = fetch_backward(owned)
        d_start, record_rows, gain_sums = backward_one(stored[micro_step], weights)
        stored[micro_step] = None
        arrived = lax.all_to_all(
            d_start[:, None, :], ("fsdp", "pair"), split_axis=0, concat_axis=1, tiled=True
        )
        input_grads[micro_step] = restore(arrived, order[micro_step])
        records[micro_step] = record_rows
        gain_totals = gain_sums if gain_totals is None else add_tuples(gain_totals, gain_sums)
    joined = tuple(
        (
            jnp.concatenate([records[step][index] for step in range(batches)], 0)
            for index in range(11)
        )
    )
    hidden1, d_query, d_keys, d_values, attended, d_branch, hidden2, d_gate, d_up, inner, d_out = (
        joined
    )
    gain_cols = jnp.stack([gain_totals[0], gain_totals[1]], 1)
    g_query, g_key, g_value, g_out, g_gains = owner_sums(
        (
            take_rows(hidden1, d_query),
            take_rows(hidden1, d_keys),
            take_rows(hidden1, d_values),
            take_rows(attended, d_branch),
            gain_cols,
        )
    )
    g_gate, g_up = owner_sums((take_rows(hidden2, d_gate), take_rows(hidden2, d_up)))
    (g_down,) = owner_sums((take_rows(inner, d_out),))
    return (
        jnp.stack(outputs),
        jnp.stack(input_grads),
        g_gains[:, 0],
        g_query,
        g_key,
        g_value,
        g_out,
        g_gains[:, 1],
        g_gate,
        g_up,
        g_down,
    )


GRID = ("z", "y", "core", "pair")
SWAP = ((0, 1), (1, 0))
LANES = 128


def swap(value, axis):
    return lax.ppermute(value, axis, SWAP)


def from_above(value, hops, size):
    return lax.ppermute(value, "z", [((i + hops) % size, i) for i in range(size)])


def after(value, *earlier):
    return lax.optimization_barrier((value, *earlier))[0]


def short(value):
    return value.astype(jnp.bfloat16)


def long(value):
    return value.astype(jnp.float32)


def matmul(left, right):
    return jnp.dot(left, right, preferred_element_type=jnp.float32)


def gather_z(block):
    return lax.all_gather(block, "z", axis=0, tiled=True)


def scatter_z(partial):
    return lax.psum_scatter(partial, "z", scatter_dimension=0, tiled=True)


def reduce_z(partial, depth):
    z = lax.axis_index("z")
    total = long(lax.dynamic_index_in_dim(partial, z, 0, False))
    for hops in range(1, depth):
        sent = lax.dynamic_index_in_dim(
            partial, lax.rem(z + depth - hops, depth), 0, False
        )
        total = total + long(from_above(sent, hops, depth))
    return total


def halves(value, index, axis):
    return (
        lax.dynamic_index_in_dim(value, index, axis, False),
        lax.dynamic_index_in_dim(value, 1 - index, axis, False),
    )


def both(mine, other, index, axis):
    return jnp.where(
        index == 0, jnp.stack([mine, other], axis), jnp.stack([other, mine], axis)
    )


def row_norm(value):
    return lax.rsqrt(jnp.mean(value * value, -1, keepdims=True) + EPSILON)


def norm_back(d_hidden, normed, scale, gain):
    d_norm = d_hidden * gain
    return scale * (d_norm - normed * jnp.mean(d_norm * normed, -1, keepdims=True))


def scores_of(query, keys, lens):
    seq_len = query.shape[1]
    features = query.shape[-1]
    scores = jnp.einsum(
        "bihe,bjhe->bhij", query, keys, preferred_element_type=jnp.float32
    ) * features ** (-0.5)
    row_ids = lax.broadcasted_iota(jnp.int32, (seq_len, seq_len), 0)
    col_ids = lax.broadcasted_iota(jnp.int32, (seq_len, seq_len), 1)
    mask = (col_ids <= row_ids)[None] & (col_ids[None] < lens[:, None, None])
    mask = mask[:, None]
    kernel = jnp.where(mask, 1.0 + scores + 0.5 * scores * scores, 0.0)
    denom = jnp.sum(kernel, -1, keepdims=True)
    return scores, mask, kernel / denom, denom


def attend(query, keys, values, lens):
    _, _, probs, _ = scores_of(query, keys, lens)
    return short(
        jnp.einsum("bhij,bjhe->bihe", short(probs), values, preferred_element_type=jnp.float32)
    )


def attend_back(query, keys, values, lens, grads):
    scores, mask, probs, denom = scores_of(query, keys, lens)
    d_probs = jnp.einsum("bihe,bjhe->bhij", grads, values, preferred_element_type=jnp.float32)
    d_values = jnp.einsum(
        "bhij,bihe->bjhe", short(probs), grads, preferred_element_type=jnp.float32
    )
    d_kernel = (d_probs - jnp.sum(d_probs * probs, -1, keepdims=True)) / denom
    d_scores = jnp.where(mask, d_kernel * (1.0 + scores), 0.0) * query.shape[-1] ** (-0.5)
    d_scores = short(d_scores)
    d_query = jnp.einsum("bhij,bjhe->bihe", d_scores, keys, preferred_element_type=jnp.float32)
    d_keys = jnp.einsum("bhij,bihe->bjhe", d_scores, query, preferred_element_type=jnp.float32)
    return short(d_query), short(d_keys), short(d_values)


def share_four(mine):
    up = swap(mine, "y")
    return jnp.concatenate([mine, up, swap(mine, "core"), swap(up, "core")], 0)


def sum_four(partial):
    count = partial.shape[0] // 4
    got = swap(partial[2 * count :], "core")
    up = short(long(partial[count : 2 * count]) + long(got[count:]))
    return long(partial[:count]) + long(got[:count]) + long(swap(up, "y"))


def share_eight(mine):
    half = mine.shape[0] // 2
    up, across = swap(mine, "y"), swap(mine, "pair")
    far_a = swap(across[:half], "y")
    far_b = swap(up[half:], "pair")
    own = [mine, up, across, far_a, far_b]
    near = [swap(mine, "core"), swap(up, "core"), swap(across, "core")]
    near += [swap(far_a, "core"), swap(far_b, "core")]
    return jnp.concatenate(own + near, 0)


def sum_eight(partial):
    count = partial.shape[0] // 8
    half = count // 2
    got = swap(partial[4 * count :], "core")
    own = long(partial[: 4 * count]) + long(got)
    far = short(own[3 * count :])
    mine, up, across = (own[i * count : (i + 1) * count] for i in range(3))
    near_a, near_b = swap(far[:half], "y"), swap(far[half:], "pair")
    across = jnp.concatenate([across[:half] + long(near_a), across[half:]], 0)
    up = jnp.concatenate([up[:half], up[half:] + long(near_b)], 0)
    return mine + long(swap(short(up), "y")) + long(swap(short(across), "pair"))


def on_grid(
    depth,
    tokens,
    cotangent,
    lengths,
    order,
    norm_gain,
    w_query,
    w_key,
    w_value,
    w_out,
    mlp_gain,
    w_gate,
    w_up,
    w_down,
):
    batches, _, seqs, width = tokens.shape
    y, core, pair = (lax.axis_index(name) for name in ("y", "core", "pair"))
    device_index = lax.axis_index(GRID)
    rows_in, hidden = w_gate.shape
    ff_rows = w_down.shape[0]
    ff_block = -(-depth * ff_rows // LANES) * LANES // depth
    fill = ff_block - ff_rows
    own_ff = depth * ff_block
    own_heads = depth
    features = w_query.shape[1] // HEADS
    head_dim = width // HEADS
    own_qk = own_heads * features

    def deal(value):
        dealt = lax.all_to_all(value, GRID, split_axis=2, concat_axis=1, tiled=True)
        return dealt.reshape(-1, width)

    def undeal(value):
        return lax.all_to_all(
            value.reshape(batches, -1, 1, width), GRID, split_axis=1, concat_axis=2, tiled=True
        )

    def spread(value, names):
        return lax.all_to_all(value, names, split_axis=0, concat_axis=0, tiled=True)

    qkv = jnp.concatenate(
        [
            weight.reshape(rows_in, depth, 4, step).transpose(2, 0, 1, 3).reshape(4, rows_in, -1)
            for weight, step in ((w_query, features), (w_key, features), (w_value, head_dim))
        ],
        2,
    )
    qkv = spread(qkv, ("y", "core"))
    start_rows = deal(after(tokens, qkv))
    gains = jnp.stack([norm_gain, mlp_gain])
    gains = spread(jnp.broadcast_to(gains[None], (seqs,) + gains.shape), GRID)
    gains = long(gains.transpose(1, 0, 2).reshape(2, 1, width))
    gain1, gain2 = gains[0], gains[1]

    def hidden_block(weight):
        cut = weight.reshape(rows_in, depth, 8, ff_rows).transpose(2, 0, 1, 3)
        cut = jnp.pad(cut, ((0, 0), (0, 0), (0, 0), (0, fill)))
        return cut.reshape(8, rows_in, own_ff)

    cut = jnp.concatenate([hidden_block(w_gate), hidden_block(w_up)], 2)
    cut = spread(cut, ("y", "core", "pair"))

    out_rows = gather_z(w_out)
    qkv_rows = gather_z(after(qkv.reshape(4 * rows_in, -1), out_rows))
    w_down_own = gather_z(after(jnp.pad(w_down, ((0, fill), (0, 0))), qkv_rows))
    gate_up = gather_z(after(cut.reshape(8 * rows_in, 2 * own_ff), w_down_own))

    def joined(mine, shape, axis):
        return both(mine.reshape(shape), swap(mine, "pair").reshape(shape), pair, axis)

    w_qkv = joined(qkv_rows, (4 * depth, rows_in, -1), 1).reshape(width, -1)
    w_out_own = joined(out_rows, (depth, rows_in, width), 1).reshape(-1, width)
    count = start_rows.shape[0]
    seq_len = count // batches

    def lens_of(device):
        return jnp.sum(jnp.where(order == device, lengths, 0), 1)

    by_core, by_y = device_index + 2 - 4 * core, 4 - 8 * y
    lens = jnp.concatenate(
        [lens_of(device_index), lens_of(device_index + by_y), lens_of(by_core), lens_of(by_core + by_y)]
    )
    start = long(start_rows)
    scale1 = row_norm(start)
    hidden1 = share_four(short(start * scale1 * gain1))
    cot_rows = deal(after(cotangent, hidden1))
    live = (
        lax.broadcasted_iota(jnp.int32, (batches, seq_len), 1) < lens[:batches, None]
    ).reshape(count, 1)
    d_out = jnp.where(live, cot_rows, jnp.zeros_like(cot_rows))
    d_out_all = share_eight(d_out)
    qkv = short(matmul(hidden1, w_qkv))
    by_seq = (4 * batches, seq_len, own_heads, -1)
    query = qkv[:, :own_qk].reshape(by_seq)
    keys = qkv[:, own_qk : 2 * own_qk].reshape(by_seq)
    values = qkv[:, 2 * own_qk :].reshape(by_seq)
    attended = attend(query, keys, values, lens).reshape(4 * count, -1)
    resid = start + sum_four(short(matmul(attended, w_out_own)))
    scale2 = row_norm(resid)
    normed2 = resid * scale2
    hidden2 = share_eight(short(normed2 * gain2))

    both_pre = matmul(hidden2, gate_up)
    gate_pre, up_pre = both_pre[:, :own_ff], both_pre[:, own_ff:]
    sigma = jax.nn.sigmoid(gate_pre)
    inner = short(gate_pre * sigma * up_pre)
    g_down = short(take_rows(inner, d_out_all))
    d_out_all, g_down = lax.optimization_barrier((d_out_all, g_down))
    g_down = scatter_z(g_down)

    d_inner = back_cols(d_out_all, w_down_own)
    d_gate = short(d_inner * up_pre * sigma * (1.0 + gate_pre * (1.0 - sigma)))
    d_up = short(d_inner * gate_pre * sigma)
    d_both = jnp.concatenate([d_gate, d_up], 1)
    d_part = short(back_cols(d_both, gate_up))
    d_both, d_part = lax.optimization_barrier((d_both, d_part))
    g_both = short(take_rows(hidden2, d_both))
    inner, g_both = lax.optimization_barrier((inner, g_both))
    g_both = scatter_z(after(g_both, g_down))
    g_down = long(g_down[:ff_rows])
    d_hidden2 = sum_eight(d_part)
    result = resid + sum_eight(short(matmul(inner, w_down_own)))
    activations = undeal(short(result))

    g_mlp = jnp.sum(d_hidden2 * normed2, 0)
    d_resid = long(d_out) + norm_back(d_hidden2, normed2, scale2, gain2)
    d_branch = share_four(short(d_resid))
    d_attended = short(back_cols(d_branch, w_out_own))

    def owned_rows(partial):
        kept, sent = halves(partial, pair, 2)
        got = swap(sent.reshape(-1, sent.shape[-1]), "pair").reshape(kept.shape)
        rows = short(long(kept) + long(got))
        return reduce_z(rows.reshape(depth, -1, rows.shape[-1]), depth)

    g_out = short(take_rows(attended, d_branch))
    g_out = owned_rows(g_out.reshape(depth, 1, 2, rows_in, width))

    d_query, d_keys, d_values = attend_back(query, keys, values, lens, d_attended.reshape(by_seq))
    d_qkv = jnp.concatenate(
        [part.reshape(4 * count, -1) for part in (d_query, d_keys, d_values)], 1
    )
    d_qkv, g_both = lax.optimization_barrier((d_qkv, g_both))
    d_hidden1 = sum_four(short(back_cols(d_qkv, w_qkv)))
    g_qkv = short(take_rows(hidden1, d_qkv))
    g_qkv = short(owned_rows(g_qkv.reshape(depth, 4, 2, rows_in, -1)))
    g_qkv = spread(g_qkv.reshape(4, rows_in, -1), ("y", "core"))
    g_both = spread(g_both.reshape(8, rows_in, -1), ("y", "core", "pair"))

    def natural(part):
        part = part.reshape(8, rows_in, depth, ff_block)[..., :ff_rows].transpose(1, 2, 0, 3)
        return long(part.reshape(rows_in, hidden))

    g_gate, g_up = natural(g_both[..., :own_ff]), natural(g_both[..., own_ff:])

    def all_heads(part, step):
        part = part.reshape(4, rows_in, depth, step).transpose(1, 2, 0, 3)
        return long(part.reshape(rows_in, -1))

    g_query = all_heads(g_qkv[..., :own_qk], features)
    g_key = all_heads(g_qkv[..., own_qk : 2 * own_qk], features)
    g_value = all_heads(g_qkv[..., 2 * own_qk :], head_dim)

    normed1 = start * scale1
    g_norm = jnp.sum(d_hidden1 * normed1, 0)
    d_start = d_resid + norm_back(d_hidden1, normed1, scale1, gain1)
    input_grad = undeal(short(d_start))

    g_gains = jnp.stack([g_norm, g_mlp]).reshape(2, seqs, rows_in).transpose(1, 0, 2)
    g_gains = jnp.sum(
        lax.all_to_all(g_gains, GRID, split_axis=0, concat_axis=0, tiled=True), 0
    )
    return (
        activations,
        input_grad,
        g_gains[0],
        g_query,
        g_key,
        g_value,
        g_out,
        g_gains[1],
        g_gate,
        g_up,
        g_down,
    )


def solution(mesh):
    fsdp, pair = mesh.shape["fsdp"], mesh.shape["pair"]
    names = ("fsdp", "pair")
    run = on_device
    if pair == 2 and fsdp == HEADS:
        names = GRID
        mesh = Mesh(mesh.devices.reshape(fsdp // 4, 2, 2, 2), GRID)
        run = functools.partial(on_grid, fsdp // 4)
    positions = P(None, names, None, None)
    rows, flat = P(names, None), P(names)
    return jax.shard_map(
        run,
        mesh=mesh,
        in_specs=(positions, positions, P(), P(), flat, rows, rows, rows, rows, flat, rows, rows, rows),
        out_specs=(positions, positions, flat, rows, rows, rows, rows, flat, rows, rows, rows),
        check_vma=False,
    )
```

```python
import functools
import math

import jax
import jax.numpy as jnp
from jax import lax
from jax.experimental import pallas as pl
from jax.experimental.pallas import tpu as pltpu
from jax.sharding import Mesh
from jax.sharding import PartitionSpec as P

HEADS = 16


PRECISE = lax.Precision.HIGHEST
EPSILON = 1e-06


def for_sending(shard):

    def short(part):
        return part.astype(jnp.bfloat16) if part.dtype == jnp.float32 else part

    return jax.tree.map(short, shard)


def take_rows(left, right):
    return lax.dot_general(
        left, right, (((0,), (0,)), ((), ())), preferred_element_type=jnp.float32
    )


def back_cols(left, right):
    return lax.dot_general(
        left, right, (((1,), (1,)), ((), ())), preferred_element_type=jnp.float32
    )


def kernel_terms(query, keys, length):
    seq_len = query.shape[0]
    features = query.shape[1] // HEADS
    query_heads = query.reshape(seq_len, HEADS, features)
    key_heads = keys.reshape(seq_len, HEADS, features)
    scores = jnp.einsum(
        "ihe,jhe->hij", query_heads, key_heads, preferred_element_type=jnp.float32
    ) * features ** (-0.5)
    row_ids = lax.broadcasted_iota(jnp.int32, (seq_len, seq_len), 0)
    col_ids = lax.broadcasted_iota(jnp.int32, (seq_len, seq_len), 1)
    key_mask = (col_ids <= row_ids) & (col_ids < length)
    kernel = jnp.where(key_mask[None], 1.0 + scores + 0.5 * scores * scores, 0.0)
    return (kernel, key_mask, scores)


def forward_one(start_rows, cot_rows, length, weights):
    norm_gain, w_query, w_key, w_value, w_out, mlp_gain, w_gate, w_up, w_down = weights
    seq_len, model_width = start_rows.shape
    start = start_rows.astype(jnp.float32)
    scale1 = lax.rsqrt(jnp.mean(start * start, -1, keepdims=True) + EPSILON)
    normed1 = start * scale1
    hidden1 = (normed1 * norm_gain.astype(jnp.float32)).astype(jnp.bfloat16)
    query = jnp.dot(hidden1, w_query, preferred_element_type=jnp.float32).astype(jnp.bfloat16)
    keys = jnp.dot(hidden1, w_key, preferred_element_type=jnp.float32).astype(jnp.bfloat16)
    values = jnp.dot(hidden1, w_value, preferred_element_type=jnp.float32).astype(jnp.bfloat16)
    kernel, key_mask, scores = kernel_terms(query, keys, length)
    denom = jnp.sum(kernel, -1)
    probs = (kernel / denom[..., None]).astype(jnp.bfloat16)
    value_heads = values.reshape(seq_len, HEADS, model_width // HEADS)
    mixed = jnp.einsum("hij,jhe->ihe", probs, value_heads, preferred_element_type=jnp.float32)
    attended = mixed.reshape(seq_len, model_width).astype(jnp.bfloat16)
    resid = start + jnp.dot(attended, w_out, preferred_element_type=jnp.float32)
    scale2 = lax.rsqrt(jnp.mean(resid * resid, -1, keepdims=True) + EPSILON)
    normed2 = resid * scale2
    hidden2 = (normed2 * mlp_gain.astype(jnp.float32)).astype(jnp.bfloat16)
    gate_pre = jnp.dot(hidden2, w_gate, preferred_element_type=jnp.float32)
    up_pre = jnp.dot(hidden2, w_up, preferred_element_type=jnp.float32)
    inner = (gate_pre * jax.nn.sigmoid(gate_pre) * up_pre).astype(jnp.bfloat16)
    result = resid + jnp.dot(inner, w_down, preferred_element_type=jnp.float32)
    saved = (
        cot_rows,
        length,
        normed1,
        scale1,
        hidden1,
        query,
        keys,
        values,
        denom,
        attended,
        normed2,
        scale2,
        hidden2,
        gate_pre,
        up_pre,
        inner,
    )
    return (result, saved)


def backward_one(saved, weights):
    norm_gain, w_query, w_key, w_value, w_out, mlp_gain, w_gate, w_up, w_down = weights
    (
        cot_rows,
        length,
        normed1,
        scale1,
        hidden1,
        query,
        keys,
        values,
        denom,
        attended,
        normed2,
        scale2,
        hidden2,
        gate_pre,
        up_pre,
        inner,
    ) = saved
    seq_len, model_width = normed1.shape
    live_rows = lax.broadcasted_iota(jnp.int32, (seq_len, 1), 0) < length
    d_out = jnp.where(live_rows, cot_rows, jnp.zeros_like(cot_rows))
    d_inner = back_cols(d_out, w_down)
    sigma = jax.nn.sigmoid(gate_pre)
    d_gate = (d_inner * up_pre * sigma * (1.0 + gate_pre * (1.0 - sigma))).astype(jnp.bfloat16)
    d_up = (d_inner * gate_pre * sigma).astype(jnp.bfloat16)
    d_hidden2 = back_cols(d_gate, w_gate) + back_cols(d_up, w_up)
    g_mlp = jnp.sum(d_hidden2 * normed2, 0)
    d_norm2 = d_hidden2 * mlp_gain.astype(jnp.float32)
    d_resid = d_out.astype(jnp.float32) + scale2 * (
        d_norm2 - normed2 * jnp.mean(d_norm2 * normed2, -1, keepdims=True)
    )
    d_branch = d_resid.astype(jnp.bfloat16)
    d_attended = back_cols(d_branch, w_out).astype(jnp.bfloat16)
    kernel, key_mask, scores = kernel_terms(query, keys, length)
    probs = kernel / denom[..., None]
    value_heads = values.reshape(seq_len, HEADS, model_width // HEADS)
    grad_heads = d_attended.reshape(seq_len, HEADS, model_width // HEADS)
    d_probs = jnp.einsum(
        "ihe,jhe->hij", grad_heads, value_heads, preferred_element_type=jnp.float32
    )
    d_values = jnp.einsum(
        "hij,ihe->jhe", probs.astype(jnp.bfloat16), grad_heads, preferred_element_type=jnp.float32
    )
    d_values = d_values.reshape(seq_len, model_width).astype(jnp.bfloat16)
    d_kernel = (d_probs - jnp.sum(d_probs * probs, -1, keepdims=True)) / denom[..., None]
    features = query.shape[1] // HEADS
    d_scores = jnp.where(key_mask[None], d_kernel * (1.0 + scores), 0.0) * features ** (-0.5)
    query_heads = query.reshape(seq_len, HEADS, features).astype(jnp.float32)
    key_heads = keys.reshape(seq_len, HEADS, features).astype(jnp.float32)
    d_query = (
        jnp.einsum("hij,jhe->ihe", d_scores, key_heads, precision=PRECISE)
        .reshape(seq_len, -1)
        .astype(jnp.bfloat16)
    )
    d_keys = (
        jnp.einsum("hij,ihe->jhe", d_scores, query_heads, precision=PRECISE)
        .reshape(seq_len, -1)
        .astype(jnp.bfloat16)
    )
    d_hidden1 = (
        back_cols(d_query, w_query) + back_cols(d_keys, w_key) + back_cols(d_values, w_value)
    )
    g_norm = jnp.sum(d_hidden1 * normed1, 0)
    d_norm1 = d_hidden1 * norm_gain.astype(jnp.float32)
    d_start = d_resid + scale1 * (
        d_norm1 - normed1 * jnp.mean(d_norm1 * normed1, -1, keepdims=True)
    )
    record_rows = (
        hidden1,
        d_query,
        d_keys,
        d_values,
        attended,
        d_branch,
        hidden2,
        d_gate,
        d_up,
        inner,
        d_out,
    )
    return (d_start.astype(jnp.bfloat16), record_rows, (g_norm, g_mlp))


def owner_sums(terms):
    arrived = jax.tree.map(
        lambda part, own: part.astype(own.dtype),
        lax.all_to_all(
            for_sending(terms), ("fsdp", "pair"), split_axis=0, concat_axis=0, tiled=True
        ),
        terms,
    )
    count = lax.axis_size(("fsdp", "pair"))
    return tuple(
        (
            jnp.sum(piece.reshape(count, piece.shape[0] // count, piece.shape[1]), 0)
            for piece in arrived
        )
    )


def restore(arrived, permuted):
    inverse = (
        jnp.zeros_like(permuted).at[permuted].set(jnp.arange(permuted.shape[0], dtype=jnp.int32))
    )
    return jnp.take(arrived, inverse, axis=1)


def fetch_backward(owned):
    return (
        lax.all_gather(owned[0], ("fsdp", "pair"), axis=0, tiled=True),
        lax.all_gather(owned[1], ("fsdp", "pair"), axis=0, tiled=True),
        lax.all_gather(owned[2], ("fsdp", "pair"), axis=0, tiled=True),
        lax.all_gather(owned[3], ("fsdp", "pair"), axis=0, tiled=True),
        lax.all_gather(owned[4], ("fsdp", "pair"), axis=0, tiled=True),
        lax.all_gather(owned[5], ("fsdp", "pair"), axis=0, tiled=True),
        lax.all_gather(owned[6], ("fsdp", "pair"), axis=0, tiled=True),
        lax.all_gather(owned[7], ("fsdp", "pair"), axis=0, tiled=True),
        lax.all_gather(owned[8], ("fsdp", "pair"), axis=0, tiled=True),
    )


def add_tuples(first_tuple, second_tuple):
    return tuple((first + second for first, second in zip(first_tuple, second_tuple)))


def on_device(
    tokens,
    cotangent,
    lengths,
    order,
    norm_gain,
    w_query,
    w_key,
    w_value,
    w_out,
    mlp_gain,
    w_gate,
    w_up,
    w_down,
):
    owned = (norm_gain, w_query, w_key, w_value, w_out, mlp_gain, w_gate, w_up, w_down)
    batches = tokens.shape[0]
    device_index = lax.axis_index(("fsdp", "pair"))
    stored = []
    outputs = []
    for micro_step in range(batches):
        weights = (
            lax.all_gather(owned[0], ("fsdp", "pair"), axis=0, tiled=True),
            lax.all_gather(owned[1], ("fsdp", "pair"), axis=0, tiled=True),
            lax.all_gather(owned[2], ("fsdp", "pair"), axis=0, tiled=True),
            lax.all_gather(owned[3], ("fsdp", "pair"), axis=0, tiled=True),
            lax.all_gather(owned[4], ("fsdp", "pair"), axis=0, tiled=True),
            lax.all_gather(owned[5], ("fsdp", "pair"), axis=0, tiled=True),
            lax.all_gather(owned[6], ("fsdp", "pair"), axis=0, tiled=True),
            lax.all_gather(owned[7], ("fsdp", "pair"), axis=0, tiled=True),
            lax.all_gather(owned[8], ("fsdp", "pair"), axis=0, tiled=True),
        )
        permuted = order[micro_step]
        dealt_tokens, dealt_cots = (
            lax.all_to_all(
                jnp.take(tokens[micro_step], permuted, axis=1),
                ("fsdp", "pair"),
                split_axis=1,
                concat_axis=0,
                tiled=True,
            ),
            lax.all_to_all(
                jnp.take(cotangent[micro_step], permuted, axis=1),
                ("fsdp", "pair"),
                split_axis=1,
                concat_axis=0,
                tiled=True,
            ),
        )
        length = lengths[micro_step][device_index]
        result, saved = forward_one(dealt_tokens[:, 0, :], dealt_cots[:, 0, :], length, weights)
        arrived = lax.all_to_all(
            result.astype(jnp.bfloat16)[:, None, :],
            ("fsdp", "pair"),
            split_axis=0,
            concat_axis=1,
            tiled=True,
        )
        outputs.append(restore(arrived, permuted))
        stored.append(saved)
    input_grads = [None] * batches
    records = [None] * batches
    gain_totals = None
    for micro_step in reversed(range(batches)):
        weights = fetch_backward(owned)
        d_start, record_rows, gain_sums = backward_one(stored[micro_step], weights)
        stored[micro_step] = None
        arrived = lax.all_to_all(
            d_start[:, None, :], ("fsdp", "pair"), split_axis=0, concat_axis=1, tiled=True
        )
        input_grads[micro_step] = restore(arrived, order[micro_step])
        records[micro_step] = record_rows
        gain_totals = gain_sums if gain_totals is None else add_tuples(gain_totals, gain_sums)
    joined = tuple(
        (
            jnp.concatenate([records[step][index] for step in range(batches)], 0)
            for index in range(11)
        )
    )
    hidden1, d_query, d_keys, d_values, attended, d_branch, hidden2, d_gate, d_up, inner, d_out = (
        joined
    )
    gain_cols = jnp.stack([gain_totals[0], gain_totals[1]], 1)
    g_query, g_key, g_value, g_out, g_gains = owner_sums(
        (
            take_rows(hidden1, d_query),
            take_rows(hidden1, d_keys),
            take_rows(hidden1, d_values),
            take_rows(attended, d_branch),
            gain_cols,
        )
    )
    g_gate, g_up = owner_sums((take_rows(hidden2, d_gate), take_rows(hidden2, d_up)))
    (g_down,) = owner_sums((take_rows(inner, d_out),))
    return (
        jnp.stack(outputs),
        jnp.stack(input_grads),
        g_gains[:, 0],
        g_query,
        g_key,
        g_value,
        g_out,
        g_gains[:, 1],
        g_gate,
        g_up,
        g_down,
    )


GRID = ("z", "y", "core", "pair")
SWAP = ((0, 1), (1, 0))
LANES = 128


def swap(value, axis):
    return lax.ppermute(value, axis, SWAP)


def from_above(value, hops, size):
    return lax.ppermute(value, "z", [((i + hops) % size, i) for i in range(size)])


def after(value, *earlier):
    return lax.optimization_barrier((value, *earlier))[0]


def short(value):
    return value.astype(jnp.bfloat16)


def long(value):
    return value.astype(jnp.float32)


def matmul(left, right):
    return jnp.dot(left, right, preferred_element_type=jnp.float32)


def gather_z(block):
    return lax.all_gather(block, "z", axis=0, tiled=True)


def scatter_z(partial):
    return lax.psum_scatter(partial, "z", scatter_dimension=0, tiled=True)


def reduce_z(partial, depth):
    z = lax.axis_index("z")
    total = long(lax.dynamic_index_in_dim(partial, z, 0, False))
    for hops in range(1, depth):
        sent = lax.dynamic_index_in_dim(
            partial, lax.rem(z + depth - hops, depth), 0, False
        )
        total = total + long(from_above(sent, hops, depth))
    return total


def halves(value, index, axis):
    return (
        lax.dynamic_index_in_dim(value, index, axis, False),
        lax.dynamic_index_in_dim(value, 1 - index, axis, False),
    )


def both(mine, other, index, axis):
    return jnp.where(
        index == 0, jnp.stack([mine, other], axis), jnp.stack([other, mine], axis)
    )


def row_norm(value):
    return lax.rsqrt(jnp.mean(value * value, -1, keepdims=True) + EPSILON)


def norm_back(d_hidden, normed, scale, gain):
    d_norm = d_hidden * gain
    return scale * (d_norm - normed * jnp.mean(d_norm * normed, -1, keepdims=True))


def scores_of(query, keys, lens):
    seq_len = query.shape[1]
    features = query.shape[-1]
    scores = jnp.einsum(
        "bihe,bjhe->bhij", query, keys, preferred_element_type=jnp.float32
    ) * features ** (-0.5)
    row_ids = lax.broadcasted_iota(jnp.int32, (seq_len, seq_len), 0)
    col_ids = lax.broadcasted_iota(jnp.int32, (seq_len, seq_len), 1)
    mask = (col_ids <= row_ids)[None] & (col_ids[None] < lens[:, None, None])
    mask = mask[:, None]
    kernel = jnp.where(mask, 1.0 + scores + 0.5 * scores * scores, 0.0)
    denom = jnp.sum(kernel, -1, keepdims=True)
    return scores, mask, kernel / denom, denom


def attend(query, keys, values, lens):
    _, _, probs, _ = scores_of(query, keys, lens)
    return short(
        jnp.einsum("bhij,bjhe->bihe", short(probs), values, preferred_element_type=jnp.float32)
    )


def attend_back(query, keys, values, lens, grads, result):
    scores, mask, probs, denom = scores_of(query, keys, lens)
    d_probs = jnp.einsum("bihe,bjhe->bhij", grads, values, preferred_element_type=jnp.float32)
    d_values = jnp.einsum(
        "bhij,bihe->bjhe", short(probs), grads, preferred_element_type=jnp.float32
    )
    d_kernel = (d_probs - jnp.sum(d_probs * probs, -1, keepdims=True)) / denom
    d_scores = jnp.where(mask, d_kernel * (1.0 + scores), 0.0) * query.shape[-1] ** (-0.5)
    d_scores, d_values, result = lax.optimization_barrier((short(d_scores), short(d_values), result))
    d_query = jnp.einsum("bhij,bjhe->bihe", d_scores, keys, preferred_element_type=jnp.float32)
    d_keys = jnp.einsum("bhij,bihe->bjhe", d_scores, query, preferred_element_type=jnp.float32)
    return short(d_query), short(d_keys), d_values, result


def share_four(mine):
    up = swap(mine, "y")
    return jnp.concatenate([mine, up, swap(mine, "core"), swap(up, "core")], 0)


def sum_four(partial):
    count = partial.shape[0] // 4
    got = swap(partial[2 * count :], "core")
    up = short(long(partial[count : 2 * count]) + long(got[count:]))
    return long(partial[:count]) + long(got[:count]) + long(swap(up, "y"))


def share_eight(mine):
    half = mine.shape[0] // 2
    up, across = swap(mine, "y"), swap(mine, "pair")
    far_a = swap(across[:half], "y")
    far_b = swap(up[half:], "pair")
    own = [mine, up, across, far_a, far_b]
    near = [swap(mine, "core"), swap(up, "core"), swap(across, "core")]
    near += [swap(far_a, "core"), swap(far_b, "core")]
    return jnp.concatenate(own + near, 0)


def sum_near(partial):
    half = partial.shape[0] // 2
    return swap(partial[half:], "core")


def sum_far(partial, got):
    count = got.shape[0] // 4
    half = count // 2
    far = short(long(partial[3 * count : 4 * count]) + long(got[3 * count :]))
    return swap(far[:half], "y"), swap(far[half:], "pair")


def sum_last(partial, got, near_a, near_b):
    count = got.shape[0] // 4
    half = count // 2

    def own(start, stop):
        return long(partial[start:stop]) + long(got[start:stop])

    up = jnp.concatenate(
        [short(own(count, count + half)), short(own(count + half, 2 * count) + long(near_b))], 0
    )
    across = jnp.concatenate(
        [short(own(2 * count, 2 * count + half) + long(near_a)), short(own(2 * count + half, 3 * count))], 0
    )
    return own(0, count) + long(swap(up, "y")) + long(swap(across, "pair"))


def on_grid(
    depth,
    tokens,
    cotangent,
    lengths,
    order,
    norm_gain,
    w_query,
    w_key,
    w_value,
    w_out,
    mlp_gain,
    w_gate,
    w_up,
    w_down,
):
    batches, _, seqs, width = tokens.shape
    y, core, pair = (lax.axis_index(name) for name in ("y", "core", "pair"))
    device_index = lax.axis_index(GRID)
    rows_in, hidden = w_gate.shape
    ff_rows = w_down.shape[0]
    ff_block = -(-depth * ff_rows // LANES) * LANES // depth
    fill = ff_block - ff_rows
    own_ff = depth * ff_block
    own_heads = depth
    features = w_query.shape[1] // HEADS
    head_dim = width // HEADS
    own_qk = own_heads * features

    def deal(value):
        dealt = lax.all_to_all(value, GRID, split_axis=2, concat_axis=1, tiled=True)
        return dealt.reshape(-1, width)

    def undeal(value):
        return lax.all_to_all(
            value.reshape(batches, -1, 1, width), GRID, split_axis=1, concat_axis=2, tiled=True
        )

    def spread(value, names):
        return lax.all_to_all(value, names, split_axis=0, concat_axis=0, tiled=True)

    qkv = jnp.concatenate(
        [
            weight.reshape(rows_in, depth, 4, step).transpose(2, 0, 1, 3).reshape(4, rows_in, -1)
            for weight, step in ((w_query, features), (w_key, features), (w_value, head_dim))
        ],
        2,
    )
    own_qkv = qkv.shape[2]
    gains = jnp.pad(jnp.stack([norm_gain, mlp_gain], 1), ((0, 0), (0, LANES - 2)))
    qkv = jnp.concatenate([qkv, jnp.broadcast_to(gains[None], (4, rows_in, LANES))], 2)
    qkv = spread(qkv, ("y", "core"))
    start_rows = deal(after(tokens, qkv))
    def hidden_block(weight):
        cut = weight.reshape(rows_in, depth, 8, ff_rows).transpose(2, 0, 1, 3)
        cut = jnp.pad(cut, ((0, 0), (0, 0), (0, 0), (0, fill)))
        return cut.reshape(8, rows_in, own_ff)

    cut = jnp.concatenate([hidden_block(w_gate), hidden_block(w_up)], 2)
    down_block = jnp.pad(w_down, ((0, fill), (0, 0)))
    start_rows, cut, down_block = lax.optimization_barrier((start_rows, cut, down_block))
    start_all = share_four(start_rows)
    cut = spread(after(cut, start_all), ("y", "core", "pair"))
    cot_rows = deal(after(cotangent, cut))

    out_rows = gather_z(w_out)
    qkv_rows = gather_z(qkv.reshape(4 * rows_in, -1))
    w_down_own = gather_z(after(down_block, qkv_rows))
    gate_up = gather_z(after(cut.reshape(8 * rows_in, 2 * own_ff), w_down_own))

    def joined(mine, shape, axis):
        return both(mine.reshape(shape), swap(mine, "pair").reshape(shape), pair, axis)

    w_qkv = joined(qkv_rows, (4 * depth, rows_in, -1), 1).reshape(width, -1)
    w_out_own = joined(out_rows, (depth, rows_in, width), 1).reshape(-1, width)
    count = start_rows.shape[0]
    seq_len = count // batches

    def lens_of(device):
        return jnp.sum(jnp.where(order == device, lengths, 0), 1)

    by_core, by_y = device_index + 2 - 4 * core, 4 - 8 * y
    lens = jnp.concatenate(
        [lens_of(device_index), lens_of(device_index + by_y), lens_of(by_core), lens_of(by_core + by_y)]
    )
    gains = long(w_qkv[:, own_qkv:].T)
    gain1, gain2 = gains[0:1], gains[1:2]
    start = long(start_all)
    scale1 = row_norm(start)
    hidden1 = short(start * scale1 * gain1)
    start, scale1 = start[:count], scale1[:count]
    qkv = short(matmul(hidden1, w_qkv))
    by_seq = (4 * batches, seq_len, own_heads, -1)
    query = qkv[:, :own_qk].reshape(by_seq)
    keys = qkv[:, own_qk : 2 * own_qk].reshape(by_seq)
    values = qkv[:, 2 * own_qk : own_qkv].reshape(by_seq)
    attended = attend(query, keys, values, lens).reshape(4 * count, -1)
    attended, cut_done = lax.optimization_barrier((attended, cut))
    resid = start + sum_four(short(matmul(attended, w_out_own)))
    scale2 = row_norm(resid)
    normed2 = resid * scale2
    hidden2 = share_eight(short(normed2 * gain2))
    live = (
        lax.broadcasted_iota(jnp.int32, (batches, seq_len), 1) < lens[:batches, None]
    ).reshape(count, 1)
    cot_rows = after(cot_rows, hidden2)
    d_out = jnp.where(live, cot_rows, jnp.zeros_like(cot_rows))
    d_out_all = share_eight(d_out)

    both_pre = matmul(hidden2, gate_up)
    gate_pre, up_pre = both_pre[:, :own_ff], both_pre[:, own_ff:]
    sigma = jax.nn.sigmoid(gate_pre)
    inner = short(gate_pre * sigma * up_pre)
    g_down = short(take_rows(inner, d_out_all))
    d_out_all, g_down = lax.optimization_barrier((d_out_all, g_down))
    g_down = scatter_z(g_down)

    d_inner = back_cols(d_out_all, w_down_own)
    d_gate = short(d_inner * up_pre * sigma * (1.0 + gate_pre * (1.0 - sigma)))
    d_up = short(d_inner * gate_pre * sigma)
    d_both = jnp.concatenate([d_gate, d_up], 1)
    d_part = short(back_cols(d_both, gate_up))
    d_both, d_part = lax.optimization_barrier((d_both, d_part))
    got = sum_near(d_part)
    g_both = short(take_rows(hidden2, d_both))
    inner, got, g_both, g_down = lax.optimization_barrier((inner, got, g_both, g_down))
    g_both = scatter_z(g_both)
    g_down = long(g_down[:ff_rows])
    d_hidden2 = sum_last(d_part, got, *sum_far(d_part, got))
    result_part = short(matmul(inner, w_down_own))
    result_got = sum_near(result_part)
    g_mlp = jnp.sum(d_hidden2 * normed2, 0)
    d_resid = long(d_out) + norm_back(d_hidden2, normed2, scale2, gain2)
    d_branch = share_four(short(d_resid))
    d_attended = short(back_cols(d_branch, w_out_own))
    d_attended, result_got = lax.optimization_barrier((d_attended, result_got))
    result_far = sum_far(result_part, result_got)
    g_out = short(take_rows(attended, d_branch))
    d_attended, g_out, result_far = lax.optimization_barrier((d_attended, g_out, result_far))
    result = short(resid + sum_last(result_part, result_got, *result_far))

    def send_over_x(partial):
        kept, sent = halves(partial, pair, 1)
        return kept, swap(sent.reshape(-1, sent.shape[-1]), "pair")

    def add_over_x(kept, got):
        total = short(long(kept) + long(got.reshape(kept.shape)))
        return total.reshape(depth, -1, kept.shape[-1])

    g_out = add_over_x(*send_over_x(g_out.reshape(depth, 2, rows_in, width)))

    d_query, d_keys, d_values, result = attend_back(
        query, keys, values, lens, d_attended.reshape(by_seq), result
    )
    d_qkv = jnp.concatenate(
        [part.reshape(4 * count, -1) for part in (d_query, d_keys, d_values)], 1
    )
    d_part = short(back_cols(jnp.pad(d_qkv, ((0, 0), (0, LANES))), w_qkv))
    d_qkv, d_part, g_both, g_out = lax.optimization_barrier((d_qkv, d_part, g_both, g_out))
    d_hidden1 = sum_four(d_part)
    g_qkv = short(take_rows(hidden1, d_qkv)).reshape(4 * depth, 2, rows_in, -1)
    kept, got = send_over_x(g_qkv)
    g_both = spread(g_both.reshape(8, rows_in, -1), ("y", "core", "pair"))
    activations = undeal(after(result, g_both))
    normed1 = start * scale1
    g_norm = jnp.sum(d_hidden1 * normed1, 0)
    d_start = short(d_resid + norm_back(d_hidden1, normed1, scale1, gain1))
    got, d_start = lax.optimization_barrier((got, d_start))
    input_grad = undeal(after(d_start, activations))
    g_qkv = short(reduce_z(add_over_x(kept, got), depth))
    g_out = reduce_z(g_out, depth)

    def trade(value, name, axis):
        index = lax.axis_index(name)
        kept, sent = halves(value, index, axis)
        got = swap(sent.reshape(-1, sent.shape[-1]), name).reshape(kept.shape)
        return both(kept, got, index, axis)

    g_qkv = trade(trade(g_qkv.reshape(2, 2, rows_in, -1), "core", 1), "y", 0)
    g_qkv = g_qkv.reshape(4, rows_in, -1)

    def natural(part):
        part = part.reshape(8, rows_in, depth, ff_block)[..., :ff_rows].transpose(1, 2, 0, 3)
        return long(part.reshape(rows_in, hidden))

    g_gate, g_up = natural(g_both[..., :own_ff]), natural(g_both[..., own_ff:])

    def all_heads(part, step):
        part = part.reshape(4, rows_in, depth, step).transpose(1, 2, 0, 3)
        return long(part.reshape(rows_in, -1))

    g_query = all_heads(g_qkv[..., :own_qk], features)
    g_key = all_heads(g_qkv[..., own_qk : 2 * own_qk], features)
    g_value = all_heads(g_qkv[..., 2 * own_qk :], head_dim)

    def swap_sum(partial, name, axis):
        kept, sent = halves(partial, lax.axis_index(name), axis)
        return kept + swap(sent, name)

    g_gains = jnp.stack([g_norm, g_mlp]).reshape(2, depth, 2, 2, 2, rows_in)
    for name, axis in (("y", 2), ("core", 2), ("pair", 2)):
        g_gains = swap_sum(g_gains, name, axis)
    g_gains = reduce_z(g_gains.transpose(1, 0, 2), depth)
    return (
        activations,
        input_grad,
        g_gains[0],
        g_query,
        g_key,
        g_value,
        g_out,
        g_gains[1],
        g_gate,
        g_up,
        g_down,
    )


def solution(mesh):
    fsdp, pair = mesh.shape["fsdp"], mesh.shape["pair"]
    names = ("fsdp", "pair")
    run = on_device
    if pair == 2 and fsdp == HEADS:
        names = GRID
        mesh = Mesh(mesh.devices.reshape(fsdp // 4, 2, 2, 2), GRID)
        run = functools.partial(on_grid, fsdp // 4)
    positions = P(None, names, None, None)
    rows, flat = P(names, None), P(names)
    return jax.shard_map(
        run,
        mesh=mesh,
        in_specs=(positions, positions, P(), P(), flat, rows, rows, rows, rows, flat, rows, rows, rows),
        out_specs=(positions, positions, flat, rows, rows, rows, rows, flat, rows, rows, rows),
        check_vma=False,
    )
```
